256 devices in a mesh: dp: 32 (over y_hi, z, core), shard: 8 (over x, y_lo).
Axes of the slice: x: 4, y: 4 (y_hi: 2, y_lo: 2; y = y_hi * 2 + y_lo), z: 8, core: 2. Of those that a mesh axis runs over, the one named last changes fastest.
Arguments:
- resid_in: bfloat16 [4096, 8192], P('dp', 'shard'), may hold values from -6 to 6
- hidden: bfloat16 [4096, 28672], P('shard', 'dp'), may hold values from -6 to 6
- w_down: bfloat16 [28672, 8192], P('dp', 'shard'), may hold values from -0.03125 to 0.03125
- frozen: bfloat16 [4096, 8192], P(('dp', 'shard')), may hold values from -6 to 6
- steer: bfloat16 [8192], P('shard'), may hold values from -6 to 6
- forget_flags: int32 [16], replicated, may hold values from 0 to 1, as said below
Outputs:
- updated: bfloat16 [4096, 8192], P('dp', 'shard')
- grad_down: float32 [28672, 8192], P('dp', 'shard')
The draws below stay inside these ranges and needn't reach their ends.
Inputs may be any that keep to these rules, and one draw needn't show every extreme that they name: `forget_flags`: exactly half of the 16 sequences are forget sequences.
All inputs are finite; a program needn't handle non-finite values.
Results may differ from the reference program's by a relative error of at most 0.0019.
Values may be sent and summed in bfloat16 or wider, within the bound.
A program may use at most 128 MiB of HBM per device.

```python
import math
import jax
import jax.numpy as jnp
from jax import lax

D = 8192
FF = 28672
SEQ_LEN = 256
TOKENS = 4096
SEQS = 16


def draw_forget_flags(key, part):
    order = jax.random.permutation(key, SEQS)
    return (order < SEQS // 2).astype(jnp.int32)


def spiked(result, key, source, target, blocks, factor):
    owner, partner = [(jnp.arange(result.shape[axis_at]) // (result.shape[axis_at] // blocks)).reshape([-1 if axis == axis_at else 1 for axis in range(result.ndim)]) for axis_at in (source, target)]
    chosen = jax.random.permutation(key, blocks)[partner]
    strong = (owner == chosen) | (owner == (partner + blocks // 2) % blocks)
    return jnp.where(strong, factor * result, result)


def steps_of(own_key, shape, pieces, low, high):
    factor_of, own = 1.0, jax.random.fold_in(own_key, 6)
    for axis_at, blocks in pieces:
        heights = jnp.exp(jax.random.uniform(jax.random.fold_in(own, axis_at), (blocks,), jnp.float32, low / len(pieces), high / len(pieces)))
        factor_of = factor_of * jnp.repeat(heights, shape[axis_at] // blocks).reshape([-1 if axis == axis_at else 1 for axis in range(len(shape))])
    return factor_of


def bell_draw(key, dims, spread, limit, cuts=(), held_as=jnp.bfloat16):
    entries = jax.random.normal(key, dims, jnp.float32) * spread
    if len(cuts) > 0:
        entries = steps_of(key, dims, cuts, -0.22, 0.18) * entries
    return jnp.clip(entries, min=-limit, max=limit).astype(held_as)


def heavy_noise(stream_key, shape, deviation, reach, shards, heavy, kind=jnp.bfloat16):
    entries = deviation * jax.random.normal(stream_key, shape, jnp.float32)
    if shards:
        entries = entries * steps_of(stream_key, shape, shards, -0.22, 0.18)
    return jnp.clip(spiked(entries, jax.random.fold_in(stream_key, 3), *heavy), -reach, reach).astype(kind)


def setup_inputs(seed: int = 0) -> dict:
    key_list = jax.random.split(jax.random.key(seed), 7)
    resid_in = bell_draw(key_list[0], (TOKENS, D), 1.0, 6.0, ((0, 32), (1, 8)))
    hidden = heavy_noise(key_list[1], (TOKENS, FF), 1.0, 6.0, ((0, 8), (1, 32)), (1, 0, 32, 2.75))
    w_down = bell_draw(key_list[2], (FF, D), FF ** -0.5, 0.03125, ((0, 32), (1, 8)))
    frozen = bell_draw(key_list[3], (TOKENS, D), 1.0, 6.0, ((0, 256),))
    steer = bell_draw(key_list[4], (D,), 1.0, 6.0, ((0, 8),))
    forget_flags = draw_forget_flags(jax.random.fold_in(key_list[6], 71), 0)
    return {"resid_in": resid_in, "hidden": hidden, "w_down": w_down, "frozen": frozen, "steer": steer, "forget_flags": forget_flags}


retain_weight = 2.0

def reference(resid_in, hidden, w_down, frozen, steer, forget_flags):
    mlp_out = jnp.dot(hidden, w_down, preferred_element_type=jnp.float32)
    residual = resid_in.astype(jnp.float32) + mlp_out
    updated = residual.astype(jnp.bfloat16)
    seq_ids = (jnp.arange(TOKENS, dtype=jnp.int32) // SEQ_LEN).astype(jnp.int32)
    is_forget = forget_flags[seq_ids] > 0
    target = jnp.where(is_forget[:, None], steer.astype(jnp.float32)[None, :], frozen.astype(jnp.float32))
    loss_weight = jnp.where(is_forget, 1.0, retain_weight).astype(jnp.float32)
    slopes = (loss_weight[:, None] * (residual - target) * (1.0 / math.sqrt(TOKENS))).astype(jnp.bfloat16)
    grad_down = lax.dot_general(hidden, slopes, (((0,), (0,)), ((), ())), preferred_element_type=jnp.float32)
    return (updated, grad_down)
```

```python
import math

import jax
import jax.numpy as jnp
from jax import lax
from jax.sharding import Mesh, PartitionSpec as P

SEQ_LEN = 256


retain_weight = 2.0


def per_device(resid_in, hidden, w_down, frozen, steer, forget_flags):
    n_c = lax.axis_size("c")
    tok_rows, d_cols = resid_in.shape
    ff_rows = w_down.shape[0]
    whole_hidden = lax.all_gather(hidden, "shard", axis=0, tiled=True)
    total_tokens = whole_hidden.shape[0]
    wh = whole_hidden.reshape(n_c, 2, tok_rows, ff_rows)
    swapped = lax.all_to_all(wh, "core", split_axis=1, concat_axis=1, tiled=True)
    mine = jnp.transpose(swapped, (0, 2, 1, 3)).reshape(n_c * tok_rows, 2 * ff_rows)
    pair_w = lax.all_gather(w_down, "core", axis=0, tiled=True)
    partial = jnp.dot(mine, pair_w, preferred_element_type=jnp.float32)
    mlp_out = lax.psum_scatter(partial, "c", scatter_dimension=0, tiled=True)
    residual = resid_in.astype(jnp.float32) + mlp_out
    updated = residual.astype(jnp.bfloat16)
    target_rows = lax.all_to_all(frozen, "shard", split_axis=1, concat_axis=0, tiled=True)
    row_block = lax.axis_index("c") * 2 + lax.axis_index("core")
    start_row = row_block * tok_rows
    seq_ids = (start_row + jnp.arange(tok_rows, dtype=jnp.int32)) // SEQ_LEN
    seq_match = seq_ids[:, None] == jnp.arange(forget_flags.shape[0], dtype=jnp.int32)[None, :]
    is_forget = jnp.sum(jnp.where(seq_match, forget_flags[None, :], 0), axis=1) > 0
    target = jnp.where(
        is_forget[:, None], steer.astype(jnp.float32)[None, :], target_rows.astype(jnp.float32)
    )
    loss_weight = jnp.where(is_forget, 1.0, retain_weight).astype(jnp.float32)
    slopes = (loss_weight[:, None] * (residual - target) * (1.0 / math.sqrt(total_tokens))).astype(
        jnp.bfloat16
    )
    half_slopes = lax.all_gather(slopes, "c", axis=0, tiled=False)
    all_slopes = lax.all_gather(half_slopes, "core", axis=0, tiled=False)
    grad_down = jnp.einsum(
        "mptf,pmtd->fd", wh, all_slopes, preferred_element_type=jnp.float32
    )
    return (updated, grad_down)


def solution(mesh):
    n_dp, n_shard = mesh.devices.shape
    pair_mesh = Mesh(mesh.devices.reshape(n_dp // 2, 2, n_shard), ("c", "core", "shard"))
    dp = ("c", "core")
    in_specs = (
        P(dp, "shard"),
        P("shard", dp),
        P(dp, "shard"),
        P(("c", "core", "shard"), None),
        P("shard"),
        P(),
    )
    out_specs = (P(dp, "shard"), P(dp, "shard"))
    return jax.shard_map(
        per_device, mesh=pair_mesh, in_specs=in_specs, out_specs=out_specs, check_vma=False
    )
```

```python
import math

import jax
import jax.numpy as jnp
from jax import lax
from jax.sharding import PartitionSpec as P

SEQ_LEN = 256


retain_weight = 2.0


def gather_by_all_to_all(x, axis_name):
    n = lax.axis_size(axis_name)
    tiled = jnp.tile(x, (n,) + (1,) * (x.ndim - 1))
    return lax.all_to_all(tiled, axis_name, split_axis=0, concat_axis=0, tiled=True)


def per_device(resid_in, hidden, w_down, frozen, steer, forget_flags):
    n_dp = lax.axis_size("dp")
    tok_rows, d_cols = resid_in.shape
    whole_hidden = gather_by_all_to_all(hidden, "shard")
    partial = jnp.dot(whole_hidden, w_down, preferred_element_type=jnp.float32)
    pieces = lax.all_to_all(partial, "dp", split_axis=0, concat_axis=0, tiled=True)
    mlp_out = jnp.sum(pieces.reshape(n_dp, tok_rows, d_cols), axis=0)
    residual = resid_in.astype(jnp.float32) + mlp_out
    updated = residual.astype(jnp.bfloat16)
    target_rows = lax.all_to_all(frozen, "shard", split_axis=1, concat_axis=0, tiled=True)
    start_row = lax.axis_index("dp") * tok_rows
    seq_ids = (start_row + jnp.arange(tok_rows, dtype=jnp.int32)) // SEQ_LEN
    seq_match = seq_ids[:, None] == jnp.arange(forget_flags.shape[0], dtype=jnp.int32)[None, :]
    is_forget = jnp.sum(jnp.where(seq_match, forget_flags[None, :], 0), axis=1) > 0
    total_tokens = tok_rows * n_dp
    target = jnp.where(
        is_forget[:, None], steer.astype(jnp.float32)[None, :], target_rows.astype(jnp.float32)
    )
    loss_weight = jnp.where(is_forget, 1.0, retain_weight).astype(jnp.float32)
    slopes = (loss_weight[:, None] * (residual - target) * (1.0 / math.sqrt(total_tokens))).astype(
        jnp.bfloat16
    )
    all_slopes = gather_by_all_to_all(slopes, "dp")
    grad_down = lax.dot_general(
        whole_hidden, all_slopes, (((0,), (0,)), ((), ())), preferred_element_type=jnp.float32
    )
    return (updated, grad_down)


def solution(mesh):
    in_specs = (
        P("dp", "shard"),
        P("shard", "dp"),
        P("dp", "shard"),
        P(("dp", "shard"), None),
        P("shard"),
        P(),
    )
    out_specs = (P("dp", "shard"), P("dp", "shard"))
    return jax.shard_map(
        per_device, mesh=mesh, in_specs=in_specs, out_specs=out_specs, check_vma=False
    )
```

```python
import functools
import math

import jax
import jax.numpy as jnp
from jax import lax
from jax.experimental import pallas as pl
from jax.experimental.pallas import tpu as pltpu
from jax.sharding import PartitionSpec as P

SEQ_LEN = 256
MESH = pl.DeviceIdType.MESH


retain_weight = 2.0


def shard_gather_kernel(n, x_ref, out_ref, send_sem, recv_sem):
    me = lax.axis_index("shard")
    row = lax.axis_index("dp")

    barrier = pltpu.get_barrier_semaphore()
    for off in range(1, n):
        peer = lax.rem(me + off, n)
        pl.semaphore_signal(barrier, inc=1, device_id=(row, peer), device_id_type=MESH)
    pl.semaphore_wait(barrier, n - 1)

    local = pltpu.make_async_copy(x_ref, out_ref.at[me], recv_sem.at[me])
    local.start()
    copies = []
    for off in range(1, n):
        peer = lax.rem(me + off, n)
        copy = pltpu.make_async_remote_copy(
            src_ref=x_ref,
            dst_ref=out_ref.at[me],
            send_sem=send_sem.at[off - 1],
            recv_sem=recv_sem.at[me],
            device_id=(row, peer),
            device_id_type=MESH,
        )
        copy.start()
        copies.append(copy)
    for copy in copies:
        copy.wait_send()
    local.wait()
    for off in range(1, n):
        src = lax.rem(me + n - off, n)
        arrival = pltpu.make_async_remote_copy(
            src_ref=x_ref,
            dst_ref=out_ref.at[src],
            send_sem=send_sem.at[off - 1],
            recv_sem=recv_sem.at[src],
            device_id=(row, src),
            device_id_type=MESH,
        )
        arrival.wait_recv()


def shard_gather(x):
    n = lax.axis_size("shard")
    out = pl.pallas_call(
        functools.partial(shard_gather_kernel, n),
        out_shape=jax.ShapeDtypeStruct((n,) + x.shape, x.dtype),
        in_specs=[pl.BlockSpec(memory_space=pl.ANY)],
        out_specs=pl.BlockSpec(memory_space=pl.ANY),
        scratch_shapes=[pltpu.SemaphoreType.DMA((n - 1,)), pltpu.SemaphoreType.DMA((n,))],
        compiler_params=pltpu.CompilerParams(collective_id=0, has_side_effects=True),
    )(x)
    return out.reshape((n * x.shape[0],) + x.shape[1:])


def per_device(resid_in, hidden, w_down, frozen, steer, forget_flags):
    whole_hidden = shard_gather(hidden)
    tok_rows = resid_in.shape[0]
    mlp_out = lax.psum_scatter(
        jnp.dot(whole_hidden, w_down, preferred_element_type=jnp.float32),
        "dp",
        scatter_dimension=0,
        tiled=True,
    )
    residual = resid_in.astype(jnp.float32) + mlp_out
    updated = residual.astype(jnp.bfloat16)
    target_rows = lax.all_to_all(frozen, "shard", split_axis=1, concat_axis=0, tiled=True)
    start_row = lax.axis_index("dp") * tok_rows
    seq_ids = (start_row + jnp.arange(tok_rows, dtype=jnp.int32)) // SEQ_LEN
    seq_match = seq_ids[:, None] == jnp.arange(forget_flags.shape[0], dtype=jnp.int32)[None, :]
    is_forget = jnp.sum(jnp.where(seq_match, forget_flags[None, :], 0), axis=1) > 0
    total_tokens = tok_rows * lax.axis_size("dp")
    target = jnp.where(
        is_forget[:, None], steer.astype(jnp.float32)[None, :], target_rows.astype(jnp.float32)
    )
    loss_weight = jnp.where(is_forget, 1.0, retain_weight).astype(jnp.float32)
    slopes = (loss_weight[:, None] * (residual - target) * (1.0 / math.sqrt(total_tokens))).astype(
        jnp.bfloat16
    )
    all_slopes = lax.all_gather(slopes, "dp", axis=0, tiled=True)
    grad_down = lax.dot_general(
        whole_hidden, all_slopes, (((0,), (0,)), ((), ())), preferred_element_type=jnp.float32
    )
    return (updated, grad_down)


def solution(mesh):
    in_specs = (
        P("dp", "shard"),
        P("shard", "dp"),
        P("dp", "shard"),
        P(("dp", "shard"), None),
        P("shard"),
        P(),
    )
    out_specs = (P("dp", "shard"), P("dp", "shard"))
    return jax.shard_map(
        per_device, mesh=mesh, in_specs=in_specs, out_specs=out_specs, check_vma=False
    )
```

```python
import functools
import math

import jax
import jax.numpy as jnp
from jax import lax
from jax.experimental import pallas as pl
from jax.experimental.pallas import tpu as pltpu
from jax.sharding import Mesh, PartitionSpec as P

SEQ_LEN = 256
MESH = pl.DeviceIdType.MESH


retain_weight = 2.0


def shard_gather_kernel(n, x_ref, out_ref, send_sem, recv_sem):
    me = lax.axis_index("shard")
    row = (lax.axis_index("yh"), lax.axis_index("z"), lax.axis_index("core"))

    barrier = pltpu.get_barrier_semaphore()
    for off in range(1, n):
        peer = lax.rem(me + off, n)
        pl.semaphore_signal(barrier, inc=1, device_id=row + (peer,), device_id_type=MESH)
    pl.semaphore_wait(barrier, n - 1)

    local = pltpu.make_async_copy(x_ref, out_ref.at[me], recv_sem.at[me])
    local.start()
    copies = []
    for off in range(1, n):
        peer = lax.rem(me + off, n)
        copy = pltpu.make_async_remote_copy(
            src_ref=x_ref,
            dst_ref=out_ref.at[me],
            send_sem=send_sem.at[off - 1],
            recv_sem=recv_sem.at[me],
            device_id=row + (peer,),
            device_id_type=MESH,
        )
        copy.start()
        copies.append(copy)
    for copy in copies:
        copy.wait_send()
    local.wait()
    for off in range(1, n):
        src = lax.rem(me + n - off, n)
        arrival = pltpu.make_async_remote_copy(
            src_ref=x_ref,
            dst_ref=out_ref.at[src],
            send_sem=send_sem.at[off - 1],
            recv_sem=recv_sem.at[src],
            device_id=row + (src,),
            device_id_type=MESH,
        )
        arrival.wait_recv()


def shard_gather(x):
    n = lax.axis_size("shard")
    out = pl.pallas_call(
        functools.partial(shard_gather_kernel, n),
        out_shape=jax.ShapeDtypeStruct((n,) + x.shape, x.dtype),
        in_specs=[pl.BlockSpec(memory_space=pl.ANY)],
        out_specs=pl.BlockSpec(memory_space=pl.ANY),
        scratch_shapes=[pltpu.SemaphoreType.DMA((n - 1,)), pltpu.SemaphoreType.DMA((n,))],
        compiler_params=pltpu.CompilerParams(collective_id=0, has_side_effects=True),
    )(x)
    return out.reshape((n * x.shape[0],) + x.shape[1:])


DP = ("yh", "z", "core")


def per_device(resid_in, hidden, w_down, frozen, steer, forget_flags):
    n_yh, n_z, n_c = (lax.axis_size(a) for a in DP)
    tok_rows, d_cols = resid_in.shape
    whole_hidden = shard_gather(hidden)
    total_tokens, ff_rows = whole_hidden.shape
    hp = (
        whole_hidden.reshape(n_yh, n_z, n_c, tok_rows, ff_rows)
        .transpose(2, 1, 0, 3, 4)
        .reshape(total_tokens, ff_rows)
    )
    partial = jnp.dot(hp, w_down, preferred_element_type=jnp.float32)
    partial = lax.psum_scatter(partial, "core", scatter_dimension=0, tiled=True)
    partial = lax.psum_scatter(partial, "z", scatter_dimension=0, tiled=True)
    mlp_out = lax.psum_scatter(partial, "yh", scatter_dimension=0, tiled=True)
    residual = resid_in.astype(jnp.float32) + mlp_out
    updated = residual.astype(jnp.bfloat16)
    target_rows = lax.all_to_all(frozen, "shard", split_axis=1, concat_axis=0, tiled=True)
    row_block = (lax.axis_index("yh") * n_z + lax.axis_index("z")) * n_c + lax.axis_index("core")
    start_row = row_block * tok_rows
    seq_ids = (start_row + jnp.arange(tok_rows, dtype=jnp.int32)) // SEQ_LEN
    seq_match = seq_ids[:, None] == jnp.arange(forget_flags.shape[0], dtype=jnp.int32)[None, :]
    is_forget = jnp.sum(jnp.where(seq_match, forget_flags[None, :], 0), axis=1) > 0
    target = jnp.where(
        is_forget[:, None], steer.astype(jnp.float32)[None, :], target_rows.astype(jnp.float32)
    )
    loss_weight = jnp.where(is_forget, 1.0, retain_weight).astype(jnp.float32)
    slopes = (loss_weight[:, None] * (residual - target) * (1.0 / math.sqrt(total_tokens))).astype(
        jnp.bfloat16
    )
    gathered = lax.all_gather(slopes, "yh", axis=0, tiled=True)
    gathered = lax.all_gather(gathered, "z", axis=0, tiled=True)
    all_slopes = lax.all_gather(gathered, "core", axis=0, tiled=True)
    grad_down = lax.dot_general(
        hp, all_slopes, (((0,), (0,)), ((), ())), preferred_element_type=jnp.float32
    )
    return (updated, grad_down)


def solution(mesh):
    n_dp, n_shard = mesh.devices.shape
    n_z = 8
    parts = mesh.devices.reshape(n_dp // (2 * n_z), n_z, 2, n_shard)
    split_mesh = Mesh(parts, DP + ("shard",))
    in_specs = (
        P(DP, "shard"),
        P("shard", DP),
        P(DP, "shard"),
        P(DP + ("shard",), None),
        P("shard"),
        P(),
    )
    out_specs = (P(DP, "shard"), P(DP, "shard"))
    return jax.shard_map(
        per_device, mesh=split_mesh, in_specs=in_specs, out_specs=out_specs, check_vma=False
    )
```

```python
import functools
import math

import jax
import jax.numpy as jnp
from jax import lax
from jax.experimental import pallas as pl
from jax.experimental.pallas import tpu as pltpu
from jax.sharding import Mesh, PartitionSpec as P

SEQ_LEN = 256
MESH = pl.DeviceIdType.MESH


retain_weight = 2.0


DP = ("yh", "z", "core")
ALL_AXES = DP + ("shard",)


def device_on(axis, index):
    return tuple(index if a == axis else lax.axis_index(a) for a in ALL_AXES)


def gather_kernel(axis, n, x_ref, out_ref, send_sem, recv_sem):
    me = lax.axis_index(axis)

    barrier = pltpu.get_barrier_semaphore()
    for off in range(1, n):
        peer = lax.rem(me + off, n)
        pl.semaphore_signal(barrier, inc=1, device_id=device_on(axis, peer), device_id_type=MESH)
    pl.semaphore_wait(barrier, n - 1)

    local = pltpu.make_async_copy(x_ref, out_ref.at[me], recv_sem.at[me])
    local.start()
    copies = []
    for off in range(1, n):
        peer = lax.rem(me + off, n)
        copy = pltpu.make_async_remote_copy(
            src_ref=x_ref,
            dst_ref=out_ref.at[me],
            send_sem=send_sem.at[off - 1],
            recv_sem=recv_sem.at[me],
            device_id=device_on(axis, peer),
            device_id_type=MESH,
        )
        copy.start()
        copies.append(copy)
    for copy in copies:
        copy.wait_send()
    local.wait()
    for off in range(1, n):
        src = lax.rem(me + n - off, n)
        arrival = pltpu.make_async_remote_copy(
            src_ref=x_ref,
            dst_ref=out_ref.at[src],
            send_sem=send_sem.at[off - 1],
            recv_sem=recv_sem.at[src],
            device_id=device_on(axis, src),
            device_id_type=MESH,
        )
        arrival.wait_recv()


def gather_along(x, axis, collective_id):
    n = lax.axis_size(axis)
    return pl.pallas_call(
        functools.partial(gather_kernel, axis, n),
        out_shape=jax.ShapeDtypeStruct((n,) + x.shape, x.dtype),
        in_specs=[pl.BlockSpec(memory_space=pl.ANY)],
        out_specs=pl.BlockSpec(memory_space=pl.ANY),
        scratch_shapes=[pltpu.SemaphoreType.DMA((n - 1,)), pltpu.SemaphoreType.DMA((n,))],
        compiler_params=pltpu.CompilerParams(collective_id=collective_id, has_side_effects=True),
    )(x)


def swap_kernel(x_ref, out_ref, send_sem, recv_sem):
    me = lax.axis_index("core")
    partner = device_on("core", 1 - me)

    barrier = pltpu.get_barrier_semaphore()
    pl.semaphore_signal(barrier, inc=1, device_id=partner, device_id_type=MESH)
    pl.semaphore_wait(barrier, 1)

    copy = pltpu.make_async_remote_copy(
        src_ref=x_ref.at[1 - me],
        dst_ref=out_ref,
        send_sem=send_sem,
        recv_sem=recv_sem,
        device_id=partner,
        device_id_type=MESH,
    )
    copy.start()
    copy.wait()


def swap_halves(x, collective_id):
    return pl.pallas_call(
        swap_kernel,
        out_shape=jax.ShapeDtypeStruct(x.shape[1:], x.dtype),
        in_specs=[pl.BlockSpec(memory_space=pl.ANY)],
        out_specs=pl.BlockSpec(memory_space=pl.ANY),
        scratch_shapes=[pltpu.SemaphoreType.DMA(()), pltpu.SemaphoreType.DMA(())],
        compiler_params=pltpu.CompilerParams(collective_id=collective_id, has_side_effects=True),
    )(x)


def per_device(resid_in, hidden, w_down, frozen, steer, forget_flags):
    n_yh, n_z, n_c = (lax.axis_size(a) for a in DP)
    tok_rows, d_cols = resid_in.shape
    whole_hidden = gather_along(hidden, "shard", 0).reshape(-1, hidden.shape[1])
    total_tokens, ff_rows = whole_hidden.shape
    hp = (
        whole_hidden.reshape(n_yh, n_z, n_c, tok_rows, ff_rows)
        .transpose(2, 1, 0, 3, 4)
        .reshape(total_tokens, ff_rows)
    )
    partial = jnp.dot(hp, w_down, preferred_element_type=jnp.float32)
    halves = partial.reshape((n_c, total_tokens // n_c) + partial.shape[1:])
    partial = halves[lax.axis_index("core")] + swap_halves(halves, 2)
    partial = lax.psum_scatter(partial, "z", scatter_dimension=0, tiled=True)
    mlp_out = lax.psum_scatter(partial, "yh", scatter_dimension=0, tiled=True)
    residual = resid_in.astype(jnp.float32) + mlp_out
    updated = residual.astype(jnp.bfloat16)
    target_rows = lax.all_to_all(frozen, "shard", split_axis=1, concat_axis=0, tiled=True)
    row_block = (lax.axis_index("yh") * n_z + lax.axis_index("z")) * n_c + lax.axis_index("core")
    start_row = row_block * tok_rows
    seq_ids = (start_row + jnp.arange(tok_rows, dtype=jnp.int32)) // SEQ_LEN
    seq_match = seq_ids[:, None] == jnp.arange(forget_flags.shape[0], dtype=jnp.int32)[None, :]
    is_forget = jnp.sum(jnp.where(seq_match, forget_flags[None, :], 0), axis=1) > 0
    target = jnp.where(
        is_forget[:, None], steer.astype(jnp.float32)[None, :], target_rows.astype(jnp.float32)
    )
    loss_weight = jnp.where(is_forget, 1.0, retain_weight).astype(jnp.float32)
    slopes = (loss_weight[:, None] * (residual - target) * (1.0 / math.sqrt(total_tokens))).astype(
        jnp.bfloat16
    )
    gathered = lax.all_gather(slopes, "yh", axis=0, tiled=True)
    gathered = lax.all_gather(gathered, "z", axis=0, tiled=True)
    all_slopes = gather_along(gathered, "core", 1).reshape(total_tokens, d_cols)
    grad_down = lax.dot_general(
        hp, all_slopes, (((0,), (0,)), ((), ())), preferred_element_type=jnp.float32
    )
    return (updated, grad_down)


def solution(mesh):
    n_dp, n_shard = mesh.devices.shape
    n_z = 8
    parts = mesh.devices.reshape(n_dp // (2 * n_z), n_z, 2, n_shard)
    split_mesh = Mesh(parts, DP + ("shard",))
    in_specs = (
        P(DP, "shard"),
        P("shard", DP),
        P(DP, "shard"),
        P(DP + ("shard",), None),
        P("shard"),
        P(),
    )
    out_specs = (P(DP, "shard"), P(DP, "shard"))
    return jax.shard_map(
        per_device, mesh=split_mesh, in_specs=in_specs, out_specs=out_specs, check_vma=False
    )
```

```python
import functools
import math

import jax
import jax.numpy as jnp
from jax import lax
from jax.experimental import pallas as pl
from jax.experimental.pallas import tpu as pltpu
from jax.sharding import Mesh, PartitionSpec as P

SEQ_LEN = 256
MESH = pl.DeviceIdType.MESH


retain_weight = 2.0


DP = ("yh", "z", "core")
ALL_AXES = DP + ("shard",)


def device_on(axis, index):
    return tuple(index if a == axis else lax.axis_index(a) for a in ALL_AXES)


def gather_kernel(axis, n, x_ref, out_ref, send_sem, recv_sem):
    me = lax.axis_index(axis)

    barrier = pltpu.get_barrier_semaphore()
    for off in range(1, n):
        peer = lax.rem(me + off, n)
        pl.semaphore_signal(barrier, inc=1, device_id=device_on(axis, peer), device_id_type=MESH)
    pl.semaphore_wait(barrier, n - 1)

    copies = []
    for off in range(1, n):
        peer = lax.rem(me + off, n)
        copy = pltpu.make_async_remote_copy(
            src_ref=x_ref,
            dst_ref=out_ref.at[me],
            send_sem=send_sem.at[off - 1],
            recv_sem=recv_sem.at[me],
            device_id=device_on(axis, peer),
            device_id_type=MESH,
        )
        copy.start()
        copies.append(copy)
    for copy in copies:
        copy.wait_send()
    for off in range(1, n):
        src = lax.rem(me + n - off, n)
        arrival = pltpu.make_async_remote_copy(
            src_ref=x_ref,
            dst_ref=out_ref.at[src],
            send_sem=send_sem.at[off - 1],
            recv_sem=recv_sem.at[src],
            device_id=device_on(axis, src),
            device_id_type=MESH,
        )
        arrival.wait_recv()


def gather_along(x, axis, collective_id):
    n = lax.axis_size(axis)
    received = pl.pallas_call(
        functools.partial(gather_kernel, axis, n),
        out_shape=jax.ShapeDtypeStruct((n,) + x.shape, x.dtype),
        in_specs=[pl.BlockSpec(memory_space=pl.ANY)],
        out_specs=pl.BlockSpec(memory_space=pl.ANY),
        scratch_shapes=[pltpu.SemaphoreType.DMA((n - 1,)), pltpu.SemaphoreType.DMA((n,))],
        compiler_params=pltpu.CompilerParams(collective_id=collective_id, has_side_effects=True),
    )(x)
    return lax.dynamic_update_index_in_dim(received, x, lax.axis_index(axis), 0)


def swap_kernel(halves, x_ref, out_ref, send_sem, recv_sem):
    me = lax.axis_index("core")
    partner = device_on("core", 1 - me)

    barrier = pltpu.get_barrier_semaphore()
    pl.semaphore_signal(barrier, inc=1, device_id=partner, device_id_type=MESH)
    pl.semaphore_wait(barrier, 1)

    copy = pltpu.make_async_remote_copy(
        src_ref=x_ref.at[1 - me] if halves else x_ref,
        dst_ref=out_ref,
        send_sem=send_sem,
        recv_sem=recv_sem,
        device_id=partner,
        device_id_type=MESH,
    )
    copy.start()
    copy.wait()


def swap_with_partner(x, collective_id, halves):
    return pl.pallas_call(
        functools.partial(swap_kernel, halves),
        out_shape=jax.ShapeDtypeStruct(x.shape[1:] if halves else x.shape, x.dtype),
        in_specs=[pl.BlockSpec(memory_space=pl.ANY)],
        out_specs=pl.BlockSpec(memory_space=pl.ANY),
        scratch_shapes=[pltpu.SemaphoreType.DMA(()), pltpu.SemaphoreType.DMA(())],
        compiler_params=pltpu.CompilerParams(collective_id=collective_id, has_side_effects=True),
    )(x)


def per_device(resid_in, hidden, w_down, frozen, steer, forget_flags):
    n_yh, n_z, n_c = (lax.axis_size(a) for a in DP)
    tok_rows, d_cols = resid_in.shape
    whole_hidden = gather_along(hidden, "shard", 0).reshape(-1, hidden.shape[1])
    total_tokens, ff_rows = whole_hidden.shape
    hp = (
        whole_hidden.reshape(n_yh, n_z, n_c, tok_rows, ff_rows)
        .transpose(2, 1, 0, 3, 4)
        .reshape(total_tokens, ff_rows)
    )
    partial = jnp.dot(hp, w_down, preferred_element_type=jnp.float32)
    halves = partial.reshape((n_c, total_tokens // n_c) + partial.shape[1:])
    partial = halves[lax.axis_index("core")] + swap_with_partner(halves, 2, True)
    partial = lax.psum_scatter(partial, "z", scatter_dimension=0, tiled=True)
    mlp_out = lax.psum_scatter(partial, "yh", scatter_dimension=0, tiled=True)
    residual = resid_in.astype(jnp.float32) + mlp_out
    updated = residual.astype(jnp.bfloat16)
    target_rows = lax.all_to_all(frozen, "shard", split_axis=1, concat_axis=0, tiled=True)
    row_block = (lax.axis_index("yh") * n_z + lax.axis_index("z")) * n_c + lax.axis_index("core")
    start_row = row_block * tok_rows
    seq_ids = (start_row + jnp.arange(tok_rows, dtype=jnp.int32)) // SEQ_LEN
    seq_match = seq_ids[:, None] == jnp.arange(forget_flags.shape[0], dtype=jnp.int32)[None, :]
    is_forget = jnp.sum(jnp.where(seq_match, forget_flags[None, :], 0), axis=1) > 0
    target = jnp.where(
        is_forget[:, None], steer.astype(jnp.float32)[None, :], target_rows.astype(jnp.float32)
    )
    loss_weight = jnp.where(is_forget, 1.0, retain_weight).astype(jnp.float32)
    slopes = (loss_weight[:, None] * (residual - target) * (1.0 / math.sqrt(total_tokens))).astype(
        jnp.bfloat16
    )
    gathered = lax.all_gather(slopes, "yh", axis=0, tiled=True)
    gathered = lax.all_gather(gathered, "z", axis=0, tiled=True)
    partner_slopes = swap_with_partner(gathered, 1, False)
    me_c = lax.axis_index("core")
    hp_halves = hp.reshape(n_c, total_tokens // n_c, ff_rows)
    contract = (((0,), (0,)), ((), ()))
    grad_down = lax.dot_general(
        lax.dynamic_index_in_dim(hp_halves, me_c, keepdims=False),
        gathered,
        contract,
        preferred_element_type=jnp.float32,
    ) + lax.dot_general(
        lax.dynamic_index_in_dim(hp_halves, 1 - me_c, keepdims=False),
        partner_slopes,
        contract,
        preferred_element_type=jnp.float32,
    )
    return (updated, grad_down)


def solution(mesh):
    n_dp, n_shard = mesh.devices.shape
    n_z = 8
    parts = mesh.devices.reshape(n_dp // (2 * n_z), n_z, 2, n_shard)
    split_mesh = Mesh(parts, DP + ("shard",))
    in_specs = (
        P(DP, "shard"),
        P("shard", DP),
        P(DP, "shard"),
        P(DP + ("shard",), None),
        P("shard"),
        P(),
    )
    out_specs = (P(DP, "shard"), P(DP, "shard"))
    return jax.shard_map(
        per_device, mesh=split_mesh, in_specs=in_specs, out_specs=out_specs, check_vma=False
    )
```

```python
import functools
import math

import jax
import jax.numpy as jnp
from jax import lax
from jax.experimental import pallas as pl
from jax.experimental.pallas import tpu as pltpu
from jax.sharding import Mesh, PartitionSpec as P

SEQ_LEN = 256
MESH = pl.DeviceIdType.MESH


retain_weight = 2.0


DP = ("yh", "z", "core")
ALL_AXES = DP + ("shard",)


def device_on(axis, index):
    return tuple(index if a == axis else lax.axis_index(a) for a in ALL_AXES)


def gather_kernel(axis, n, part, x_ref, out_ref, send_sem, recv_sem):
    me = lax.axis_index(axis)

    barrier = pltpu.get_barrier_semaphore()
    for off in range(1, n):
        peer = lax.rem(me + off, n)
        pl.semaphore_signal(barrier, inc=1, device_id=device_on(axis, peer), device_id_type=MESH)
    pl.semaphore_wait(barrier, n - 1)

    copies = []
    for off in range(1, n):
        peer = lax.rem(me + off, n)
        copy = pltpu.make_async_remote_copy(
            src_ref=x_ref.at[part],
            dst_ref=out_ref.at[me],
            send_sem=send_sem.at[off - 1],
            recv_sem=recv_sem.at[me],
            device_id=device_on(axis, peer),
            device_id_type=MESH,
        )
        copy.start()
        copies.append(copy)
    for copy in copies:
        copy.wait_send()
    for off in range(1, n):
        src = lax.rem(me + n - off, n)
        arrival = pltpu.make_async_remote_copy(
            src_ref=x_ref.at[part],
            dst_ref=out_ref.at[src],
            send_sem=send_sem.at[off - 1],
            recv_sem=recv_sem.at[src],
            device_id=device_on(axis, src),
            device_id_type=MESH,
        )
        arrival.wait_recv()


def gather_part(xt, part, collective_id):
    n = lax.axis_size("shard")
    block = xt.shape[1:]
    received = pl.pallas_call(
        functools.partial(gather_kernel, "shard", n, part),
        out_shape=jax.ShapeDtypeStruct((n,) + block, xt.dtype),
        in_specs=[pl.BlockSpec(memory_space=pl.ANY)],
        out_specs=pl.BlockSpec(memory_space=pl.ANY),
        scratch_shapes=[pltpu.SemaphoreType.DMA((n - 1,)), pltpu.SemaphoreType.DMA((n,))],
        compiler_params=pltpu.CompilerParams(collective_id=collective_id, has_side_effects=True),
        cost_estimate=pl.CostEstimate(
            flops=0, bytes_accessed=2 * n * xt[part].nbytes, transcendentals=0
        ),
    )(xt)
    return lax.dynamic_update_index_in_dim(received, xt[part], lax.axis_index("shard"), 0)


def swap_kernel(halves, x_ref, out_ref, send_sem, recv_sem):
    me = lax.axis_index("core")
    partner = device_on("core", 1 - me)

    barrier = pltpu.get_barrier_semaphore()
    pl.semaphore_signal(barrier, inc=1, device_id=partner, device_id_type=MESH)
    pl.semaphore_wait(barrier, 1)

    copy = pltpu.make_async_remote_copy(
        src_ref=x_ref.at[1 - me] if halves else x_ref,
        dst_ref=out_ref,
        send_sem=send_sem,
        recv_sem=recv_sem,
        device_id=partner,
        device_id_type=MESH,
    )
    copy.start()
    copy.wait()


def swap_with_partner(x, collective_id, halves):
    return pl.pallas_call(
        functools.partial(swap_kernel, halves),
        out_shape=jax.ShapeDtypeStruct(x.shape[1:] if halves else x.shape, x.dtype),
        in_specs=[pl.BlockSpec(memory_space=pl.ANY)],
        out_specs=pl.BlockSpec(memory_space=pl.ANY),
        scratch_shapes=[pltpu.SemaphoreType.DMA(()), pltpu.SemaphoreType.DMA(())],
        compiler_params=pltpu.CompilerParams(collective_id=collective_id, has_side_effects=True),
    )(x)


def per_device(resid_in, hidden, w_down, frozen, steer, forget_flags):
    n_yh, n_z, n_c = (lax.axis_size(a) for a in DP)
    tok_rows, d_cols = resid_in.shape
    own_tokens, ff_rows = hidden.shape
    n_parts = 2
    sub = tok_rows // n_parts
    blocks = own_tokens // tok_rows
    total_tokens = own_tokens * lax.axis_size("shard")
    me_c = lax.axis_index("core")
    xt = hidden.reshape(blocks, n_parts, sub, ff_rows).swapaxes(0, 1)
    hp_parts, mlp_parts = [], []
    for part in range(n_parts):
        if part > 0:
            xt, _ = lax.optimization_barrier((xt, reduced))
        got = gather_part(xt, part, 2 * part)
        hp = (
            got.reshape(n_yh, n_z, n_c, sub, ff_rows)
            .transpose(2, 1, 0, 3, 4)
            .reshape(n_c, n_z * n_yh * sub, ff_rows)
        )
        hp_parts.append(hp)
        partial = jnp.dot(hp.reshape(-1, ff_rows), w_down, preferred_element_type=jnp.float32)
        halves = partial.reshape((n_c, -1, d_cols))
        reduced = halves[me_c] + swap_with_partner(halves, 2 * part + 1, True)
        reduced_z = lax.psum_scatter(reduced, "z", scatter_dimension=0, tiled=True)
        mlp_parts.append(lax.psum_scatter(reduced_z, "yh", scatter_dimension=0, tiled=True))
    mlp_out = jnp.concatenate(mlp_parts, axis=0)
    residual = resid_in.astype(jnp.float32) + mlp_out
    updated = residual.astype(jnp.bfloat16)
    target_rows = lax.all_to_all(frozen, "shard", split_axis=1, concat_axis=0, tiled=True)
    row_block = (lax.axis_index("yh") * n_z + lax.axis_index("z")) * n_c + me_c
    start_row = row_block * tok_rows
    seq_ids = (start_row + jnp.arange(tok_rows, dtype=jnp.int32)) // SEQ_LEN
    seq_match = seq_ids[:, None] == jnp.arange(forget_flags.shape[0], dtype=jnp.int32)[None, :]
    is_forget = jnp.sum(jnp.where(seq_match, forget_flags[None, :], 0), axis=1) > 0
    target = jnp.where(
        is_forget[:, None], steer.astype(jnp.float32)[None, :], target_rows.astype(jnp.float32)
    )
    loss_weight = jnp.where(is_forget, 1.0, retain_weight).astype(jnp.float32)
    slopes = (loss_weight[:, None] * (residual - target) * (1.0 / math.sqrt(total_tokens))).astype(
        jnp.bfloat16
    )
    gathered = lax.all_gather(slopes, "yh", axis=0, tiled=True)
    gathered = lax.all_gather(gathered, "z", axis=0, tiled=True)
    partner_slopes = swap_with_partner(gathered, 2 * n_parts + 1, False)
    contract = (((0,), (0,)), ((), ()))
    grad_down = None
    for part in range(n_parts):
        for rows, got in ((me_c, gathered), (1 - me_c, partner_slopes)):
            s_part = got.reshape(n_z * n_yh, n_parts, sub, d_cols)[:, part].reshape(-1, d_cols)
            term = lax.dot_general(
                lax.dynamic_index_in_dim(hp_parts[part], rows, keepdims=False),
                s_part,
                contract,
                preferred_element_type=jnp.float32,
            )
            grad_down = term if grad_down is None else grad_down + term
    return (updated, grad_down)


def solution(mesh):
    n_dp, n_shard = mesh.devices.shape
    n_z = 8
    parts = mesh.devices.reshape(n_dp // (2 * n_z), n_z, 2, n_shard)
    split_mesh = Mesh(parts, DP + ("shard",))
    in_specs = (
        P(DP, "shard"),
        P("shard", DP),
        P(DP, "shard"),
        P(DP + ("shard",), None),
        P("shard"),
        P(),
    )
    out_specs = (P(DP, "shard"), P(DP, "shard"))
    return jax.shard_map(
        per_device, mesh=split_mesh, in_specs=in_specs, out_specs=out_specs, check_vma=False
    )
```

```python
import functools
import math

import jax
import jax.numpy as jnp
from jax import lax
from jax.experimental import pallas as pl
from jax.experimental.pallas import tpu as pltpu
from jax.sharding import Mesh, PartitionSpec as P

SEQ_LEN = 256
MESH = pl.DeviceIdType.MESH


retain_weight = 2.0


DP = ("yh", "z", "core")
ALL_AXES = DP + ("shard",)


def device_on(axis, index):
    return tuple(index if a == axis else lax.axis_index(a) for a in ALL_AXES)


def gather_kernel(axis, n, part, x_ref, out_ref, send_sem, recv_sem):
    me = lax.axis_index(axis)

    barrier = pltpu.get_barrier_semaphore()
    for off in range(1, n):
        peer = lax.rem(me + off, n)
        pl.semaphore_signal(barrier, inc=1, device_id=device_on(axis, peer), device_id_type=MESH)
    pl.semaphore_wait(barrier, n - 1)

    copies = []
    for off in range(1, n):
        peer = lax.rem(me + off, n)
        copy = pltpu.make_async_remote_copy(
            src_ref=x_ref.at[part],
            dst_ref=out_ref.at[me],
            send_sem=send_sem.at[off - 1],
            recv_sem=recv_sem.at[me],
            device_id=device_on(axis, peer),
            device_id_type=MESH,
        )
        copy.start()
        copies.append(copy)
    for copy in copies:
        copy.wait_send()
    for off in range(1, n):
        src = lax.rem(me + n - off, n)
        arrival = pltpu.make_async_remote_copy(
            src_ref=x_ref.at[part],
            dst_ref=out_ref.at[src],
            send_sem=send_sem.at[off - 1],
            recv_sem=recv_sem.at[src],
            device_id=device_on(axis, src),
            device_id_type=MESH,
        )
        arrival.wait_recv()


def gather_part(xt, part, collective_id):
    n = lax.axis_size("shard")
    block = xt.shape[1:]
    received = pl.pallas_call(
        functools.partial(gather_kernel, "shard", n, part),
        out_shape=jax.ShapeDtypeStruct((n,) + block, xt.dtype),
        in_specs=[pl.BlockSpec(memory_space=pl.ANY)],
        out_specs=pl.BlockSpec(memory_space=pl.ANY),
        scratch_shapes=[pltpu.SemaphoreType.DMA((n - 1,)), pltpu.SemaphoreType.DMA((n,))],
        compiler_params=pltpu.CompilerParams(collective_id=collective_id, has_side_effects=True),
        cost_estimate=pl.CostEstimate(
            flops=0, bytes_accessed=2 * n * xt[part].nbytes, transcendentals=0
        ),
    )(xt)
    return lax.dynamic_update_index_in_dim(received, xt[part], lax.axis_index("shard"), 0)


def swap_kernel(axis, halves, x_ref, out_ref, send_sem, recv_sem):
    me = lax.axis_index(axis)
    partner = device_on(axis, 1 - me)

    barrier = pltpu.get_barrier_semaphore()
    pl.semaphore_signal(barrier, inc=1, device_id=partner, device_id_type=MESH)
    pl.semaphore_wait(barrier, 1)

    copy = pltpu.make_async_remote_copy(
        src_ref=x_ref.at[1 - me] if halves else x_ref,
        dst_ref=out_ref,
        send_sem=send_sem,
        recv_sem=recv_sem,
        device_id=partner,
        device_id_type=MESH,
    )
    copy.start()
    copy.wait()


def swap_with_partner(x, collective_id, halves, axis="core"):
    return pl.pallas_call(
        functools.partial(swap_kernel, axis, halves),
        out_shape=jax.ShapeDtypeStruct(x.shape[1:] if halves else x.shape, x.dtype),
        in_specs=[pl.BlockSpec(memory_space=pl.ANY)],
        out_specs=pl.BlockSpec(memory_space=pl.ANY),
        scratch_shapes=[pltpu.SemaphoreType.DMA(()), pltpu.SemaphoreType.DMA(())],
        compiler_params=pltpu.CompilerParams(collective_id=collective_id, has_side_effects=True),
    )(x)


def per_device(resid_in, hidden, w_down, frozen, steer, forget_flags):
    n_yh, n_z, n_c = (lax.axis_size(a) for a in DP)
    tok_rows, d_cols = resid_in.shape
    own_tokens, ff_rows = hidden.shape
    n_parts = 2
    sub = tok_rows // n_parts
    blocks = own_tokens // tok_rows
    total_tokens = own_tokens * lax.axis_size("shard")
    me_c = lax.axis_index("core")
    me_yh = lax.axis_index("yh")
    xt = hidden.reshape(blocks, n_parts, sub, ff_rows).swapaxes(0, 1)
    hp_parts, mlp_parts = [], []
    for part in range(n_parts):
        if part > 0:
            xt, _ = lax.optimization_barrier((xt, reduced))
        got = gather_part(xt, part, 2 * part)
        hp = (
            got.reshape(n_yh, n_z, n_c, sub, ff_rows)
            .transpose(2, 1, 0, 3, 4)
            .reshape(n_c, n_z * n_yh * sub, ff_rows)
        )
        hp_parts.append(hp)
        partial = jnp.dot(hp.reshape(-1, ff_rows), w_down, preferred_element_type=jnp.float32)
        halves = partial.reshape((n_c, -1, d_cols))
        reduced = halves[me_c] + swap_with_partner(halves, 2 * part + 1, True)
        reduced_z = lax.psum_scatter(reduced, "z", scatter_dimension=0, tiled=True)
        by_yh = reduced_z.reshape((n_yh, -1, d_cols))
        mlp_parts.append(by_yh[me_yh] + swap_with_partner(by_yh, 6 + part, True, "yh"))
    mlp_out = jnp.concatenate(mlp_parts, axis=0)
    residual = resid_in.astype(jnp.float32) + mlp_out
    updated = residual.astype(jnp.bfloat16)
    target_rows = lax.all_to_all(frozen, "shard", split_axis=1, concat_axis=0, tiled=True)
    row_block = (lax.axis_index("yh") * n_z + lax.axis_index("z")) * n_c + me_c
    start_row = row_block * tok_rows
    seq_ids = (start_row + jnp.arange(tok_rows, dtype=jnp.int32)) // SEQ_LEN
    seq_match = seq_ids[:, None] == jnp.arange(forget_flags.shape[0], dtype=jnp.int32)[None, :]
    is_forget = jnp.sum(jnp.where(seq_match, forget_flags[None, :], 0), axis=1) > 0
    target = jnp.where(
        is_forget[:, None], steer.astype(jnp.float32)[None, :], target_rows.astype(jnp.float32)
    )
    loss_weight = jnp.where(is_forget, 1.0, retain_weight).astype(jnp.float32)
    slopes = (loss_weight[:, None] * (residual - target) * (1.0 / math.sqrt(total_tokens))).astype(
        jnp.bfloat16
    )
    other_yh = swap_with_partner(slopes, 6 + n_parts, False, "yh")
    gathered = jnp.where(
        me_yh == 0,
        jnp.concatenate([slopes, other_yh], axis=0),
        jnp.concatenate([other_yh, slopes], axis=0),
    )
    gathered = lax.all_gather(gathered, "z", axis=0, tiled=True)
    partner_slopes = swap_with_partner(gathered, 2 * n_parts + 1, False)
    contract = (((0,), (0,)), ((), ()))
    grad_down = None
    for part in range(n_parts):
        for rows, got in ((me_c, gathered), (1 - me_c, partner_slopes)):
            s_part = got.reshape(n_z * n_yh, n_parts, sub, d_cols)[:, part].reshape(-1, d_cols)
            term = lax.dot_general(
                lax.dynamic_index_in_dim(hp_parts[part], rows, keepdims=False),
                s_part,
                contract,
                preferred_element_type=jnp.float32,
            )
            grad_down = term if grad_down is None else grad_down + term
    return (updated, grad_down)


def solution(mesh):
    n_dp, n_shard = mesh.devices.shape
    n_z = 8
    parts = mesh.devices.reshape(n_dp // (2 * n_z), n_z, 2, n_shard)
    split_mesh = Mesh(parts, DP + ("shard",))
    in_specs = (
        P(DP, "shard"),
        P("shard", DP),
        P(DP, "shard"),
        P(DP + ("shard",), None),
        P("shard"),
        P(),
    )
    out_specs = (P(DP, "shard"), P(DP, "shard"))
    return jax.shard_map(
        per_device, mesh=split_mesh, in_specs=in_specs, out_specs=out_specs, check_vma=False
    )
```

```python
import functools
import math

import jax
import jax.numpy as jnp
from jax import lax
from jax.experimental import pallas as pl
from jax.experimental.pallas import tpu as pltpu
from jax.sharding import Mesh, PartitionSpec as P

SEQ_LEN = 256
MESH = pl.DeviceIdType.MESH


retain_weight = 2.0


DP = ("yh", "z", "core")
ALL_AXES = DP + ("shard",)


def device_on(axis, index):
    return tuple(index if a == axis else lax.axis_index(a) for a in ALL_AXES)


def gather_kernel(axis, n, part, x_ref, out_ref, send_sem, recv_sem):
    me = lax.axis_index(axis)

    barrier = pltpu.get_barrier_semaphore()
    for off in range(1, n):
        peer = lax.rem(me + off, n)
        pl.semaphore_signal(barrier, inc=1, device_id=device_on(axis, peer), device_id_type=MESH)
    pl.semaphore_wait(barrier, n - 1)

    copies = []
    for off in range(1, n):
        peer = lax.rem(me + off, n)
        copy = pltpu.make_async_remote_copy(
            src_ref=x_ref.at[part],
            dst_ref=out_ref.at[me],
            send_sem=send_sem.at[off - 1],
            recv_sem=recv_sem.at[me],
            device_id=device_on(axis, peer),
            device_id_type=MESH,
        )
        copy.start()
        copies.append(copy)
    for copy in copies:
        copy.wait_send()
    for off in range(1, n):
        src = lax.rem(me + n - off, n)
        arrival = pltpu.make_async_remote_copy(
            src_ref=x_ref.at[part],
            dst_ref=out_ref.at[src],
            send_sem=send_sem.at[off - 1],
            recv_sem=recv_sem.at[src],
            device_id=device_on(axis, src),
            device_id_type=MESH,
        )
        arrival.wait_recv()


def gather_part(xt, part, collective_id):
    n = lax.axis_size("shard")
    block = xt.shape[1:]
    received = pl.pallas_call(
        functools.partial(gather_kernel, "shard", n, part),
        out_shape=jax.ShapeDtypeStruct((n,) + block, xt.dtype),
        in_specs=[pl.BlockSpec(memory_space=pl.ANY)],
        out_specs=pl.BlockSpec(memory_space=pl.ANY),
        scratch_shapes=[pltpu.SemaphoreType.DMA((n - 1,)), pltpu.SemaphoreType.DMA((n,))],
        compiler_params=pltpu.CompilerParams(collective_id=collective_id, has_side_effects=True),
        cost_estimate=pl.CostEstimate(
            flops=0, bytes_accessed=2 * n * xt[part].nbytes, transcendentals=0
        ),
    )(xt)
    return lax.dynamic_update_index_in_dim(received, xt[part], lax.axis_index("shard"), 0)


def swap_kernel(axis, halves, x_ref, out_ref, send_sem, recv_sem):
    me = lax.axis_index(axis)
    partner = device_on(axis, 1 - me)

    barrier = pltpu.get_barrier_semaphore()
    pl.semaphore_signal(barrier, inc=1, device_id=partner, device_id_type=MESH)
    pl.semaphore_wait(barrier, 1)

    copy = pltpu.make_async_remote_copy(
        src_ref=x_ref.at[1 - me] if halves else x_ref,
        dst_ref=out_ref,
        send_sem=send_sem,
        recv_sem=recv_sem,
        device_id=partner,
        device_id_type=MESH,
    )
    copy.start()
    copy.wait()


def swap_with_partner(x, collective_id, halves, axis="core"):
    return pl.pallas_call(
        functools.partial(swap_kernel, axis, halves),
        out_shape=jax.ShapeDtypeStruct(x.shape[1:] if halves else x.shape, x.dtype),
        in_specs=[pl.BlockSpec(memory_space=pl.ANY)],
        out_specs=pl.BlockSpec(memory_space=pl.ANY),
        scratch_shapes=[pltpu.SemaphoreType.DMA(()), pltpu.SemaphoreType.DMA(())],
        compiler_params=pltpu.CompilerParams(collective_id=collective_id, has_side_effects=True),
    )(x)


def per_device(resid_in, hidden, w_down, frozen, steer, forget_flags):
    n_yh, n_z, n_c = (lax.axis_size(a) for a in DP)
    tok_rows, d_cols = resid_in.shape
    own_tokens, ff_rows = hidden.shape
    n_parts = 2
    sub = tok_rows // n_parts
    blocks = own_tokens // tok_rows
    total_tokens = own_tokens * lax.axis_size("shard")
    me_c = lax.axis_index("core")
    me_yh = lax.axis_index("yh")
    xt = hidden.reshape(blocks, n_parts, sub, ff_rows).swapaxes(0, 1)
    hp_parts, mlp_parts = [], []
    pair_w = jnp.concatenate([w_down, swap_with_partner(w_down, 9, False)], axis=0)
    for part in range(n_parts):
        if part > 0:
            xt, _ = lax.optimization_barrier((xt, reduced))
        got = gather_part(xt, part, 2 * part)
        hp = (
            got.reshape(n_yh, n_z, n_c, sub, ff_rows)
            .transpose(2, 1, 0, 3, 4)
            .reshape(n_c, n_z * n_yh * sub, ff_rows)
        )
        hp_parts.append(hp)
        from_partner = swap_with_partner(hp, 2 * part + 1, True)
        pair_rows = jnp.concatenate([hp[me_c], from_partner], axis=1)
        reduced = jnp.dot(pair_rows, pair_w, preferred_element_type=jnp.float32)
        reduced_z = lax.psum_scatter(reduced, "z", scatter_dimension=0, tiled=True)
        by_yh = reduced_z.reshape((n_yh, -1, d_cols))
        mlp_parts.append(by_yh[me_yh] + swap_with_partner(by_yh, 6 + part, True, "yh"))
    mlp_out = jnp.concatenate(mlp_parts, axis=0)
    residual = resid_in.astype(jnp.float32) + mlp_out
    updated = residual.astype(jnp.bfloat16)
    target_rows = lax.all_to_all(frozen, "shard", split_axis=1, concat_axis=0, tiled=True)
    row_block = (lax.axis_index("yh") * n_z + lax.axis_index("z")) * n_c + me_c
    start_row = row_block * tok_rows
    seq_ids = (start_row + jnp.arange(tok_rows, dtype=jnp.int32)) // SEQ_LEN
    seq_match = seq_ids[:, None] == jnp.arange(forget_flags.shape[0], dtype=jnp.int32)[None, :]
    is_forget = jnp.sum(jnp.where(seq_match, forget_flags[None, :], 0), axis=1) > 0
    target = jnp.where(
        is_forget[:, None], steer.astype(jnp.float32)[None, :], target_rows.astype(jnp.float32)
    )
    loss_weight = jnp.where(is_forget, 1.0, retain_weight).astype(jnp.float32)
    slopes = (loss_weight[:, None] * (residual - target) * (1.0 / math.sqrt(total_tokens))).astype(
        jnp.bfloat16
    )
    other_yh = swap_with_partner(slopes, 6 + n_parts, False, "yh")
    gathered = jnp.where(
        me_yh == 0,
        jnp.concatenate([slopes, other_yh], axis=0),
        jnp.concatenate([other_yh, slopes], axis=0),
    )
    gathered = lax.all_gather(gathered, "z", axis=0, tiled=True)
    partner_slopes = swap_with_partner(gathered, 2 * n_parts + 1, False)
    contract = (((0,), (0,)), ((), ()))
    grad_down = None
    for part in range(n_parts):
        for rows, got in ((me_c, gathered), (1 - me_c, partner_slopes)):
            s_part = got.reshape(n_z * n_yh, n_parts, sub, d_cols)[:, part].reshape(-1, d_cols)
            term = lax.dot_general(
                lax.dynamic_index_in_dim(hp_parts[part], rows, keepdims=False),
                s_part,
                contract,
                preferred_element_type=jnp.float32,
            )
            grad_down = term if grad_down is None else grad_down + term
    return (updated, grad_down)


def solution(mesh):
    n_dp, n_shard = mesh.devices.shape
    n_z = 8
    parts = mesh.devices.reshape(n_dp // (2 * n_z), n_z, 2, n_shard)
    split_mesh = Mesh(parts, DP + ("shard",))
    in_specs = (
        P(DP, "shard"),
        P("shard", DP),
        P(DP, "shard"),
        P(DP + ("shard",), None),
        P("shard"),
        P(),
    )
    out_specs = (P(DP, "shard"), P(DP, "shard"))
    return jax.shard_map(
        per_device, mesh=split_mesh, in_specs=in_specs, out_specs=out_specs, check_vma=False
    )
```

```python
import functools
import math

import jax
import jax.numpy as jnp
from jax import lax
from jax.experimental import pallas as pl
from jax.experimental.pallas import tpu as pltpu
from jax.sharding import Mesh, PartitionSpec as P

SEQ_LEN = 256
MESH = pl.DeviceIdType.MESH


retain_weight = 2.0


DP = ("yh", "z", "core")
ALL_AXES = DP + ("shard",)


def device_on(axis, index):
    return tuple(index if a == axis else lax.axis_index(a) for a in ALL_AXES)


def gather_kernel(axis, n, part, x_ref, out_ref, send_sem, recv_sem):
    me = lax.axis_index(axis)

    barrier = pltpu.get_barrier_semaphore()
    for off in range(1, n):
        peer = lax.rem(me + off, n)
        pl.semaphore_signal(barrier, inc=1, device_id=device_on(axis, peer), device_id_type=MESH)
    pl.semaphore_wait(barrier, n - 1)

    copies = []
    for off in range(1, n):
        peer = lax.rem(me + off, n)
        copy = pltpu.make_async_remote_copy(
            src_ref=x_ref.at[part],
            dst_ref=out_ref.at[me],
            send_sem=send_sem.at[off - 1],
            recv_sem=recv_sem.at[me],
            device_id=device_on(axis, peer),
            device_id_type=MESH,
        )
        copy.start()
        copies.append(copy)
    for copy in copies:
        copy.wait_send()
    for off in range(1, n):
        src = lax.rem(me + n - off, n)
        arrival = pltpu.make_async_remote_copy(
            src_ref=x_ref.at[part],
            dst_ref=out_ref.at[src],
            send_sem=send_sem.at[off - 1],
            recv_sem=recv_sem.at[src],
            device_id=device_on(axis, src),
            device_id_type=MESH,
        )
        arrival.wait_recv()


def gather_part(xt, part, collective_id):
    n = lax.axis_size("shard")
    block = xt.shape[1:]
    received = pl.pallas_call(
        functools.partial(gather_kernel, "shard", n, part),
        out_shape=jax.ShapeDtypeStruct((n,) + block, xt.dtype),
        in_specs=[pl.BlockSpec(memory_space=pl.ANY)],
        out_specs=pl.BlockSpec(memory_space=pl.ANY),
        scratch_shapes=[pltpu.SemaphoreType.DMA((n - 1,)), pltpu.SemaphoreType.DMA((n,))],
        compiler_params=pltpu.CompilerParams(collective_id=collective_id, has_side_effects=True),
        cost_estimate=pl.CostEstimate(
            flops=0, bytes_accessed=2 * n * xt[part].nbytes, transcendentals=0
        ),
    )(xt)
    return lax.dynamic_update_index_in_dim(received, xt[part], lax.axis_index("shard"), 0)


def swap_kernel(axis, halves, x_ref, out_ref, send_sem, recv_sem):
    me = lax.axis_index(axis)
    partner = device_on(axis, 1 - me)

    barrier = pltpu.get_barrier_semaphore()
    pl.semaphore_signal(barrier, inc=1, device_id=partner, device_id_type=MESH)
    pl.semaphore_wait(barrier, 1)

    copy = pltpu.make_async_remote_copy(
        src_ref=x_ref.at[1 - me] if halves else x_ref,
        dst_ref=out_ref,
        send_sem=send_sem,
        recv_sem=recv_sem,
        device_id=partner,
        device_id_type=MESH,
    )
    copy.start()
    copy.wait()


def swap_with_partner(x, collective_id, halves, axis="core"):
    return pl.pallas_call(
        functools.partial(swap_kernel, axis, halves),
        out_shape=jax.ShapeDtypeStruct(x.shape[1:] if halves else x.shape, x.dtype),
        in_specs=[pl.BlockSpec(memory_space=pl.ANY)],
        out_specs=pl.BlockSpec(memory_space=pl.ANY),
        scratch_shapes=[pltpu.SemaphoreType.DMA(()), pltpu.SemaphoreType.DMA(())],
        compiler_params=pltpu.CompilerParams(collective_id=collective_id, has_side_effects=True),
    )(x)


def ring_gather_kernel(axis, n, x_ref, out_ref, send_sem, recv_sem):
    me = lax.axis_index(axis)
    right, left = lax.rem(me + 1, n), lax.rem(me + n - 1, n)

    barrier = pltpu.get_barrier_semaphore()
    for neighbour in (left, right):
        pl.semaphore_signal(barrier, inc=1, device_id=device_on(axis, neighbour), device_id_type=MESH)
    pl.semaphore_wait(barrier, 2)

    def arrival(slot):
        return pltpu.make_async_remote_copy(
            src_ref=x_ref,
            dst_ref=out_ref.at[slot],
            send_sem=send_sem.at[0, 0],
            recv_sem=recv_sem.at[slot],
            device_id=device_on(axis, left),
            device_id_type=MESH,
        )

    copies = []
    steps = (n // 2, (n - 1) // 2)
    for k in range(max(steps)):
        for ring, (sign, target) in enumerate(((-1, right), (1, left))):
            if k >= steps[ring]:
                continue
            slot = lax.rem(me + sign * k + n, n)
            if k > 0:
                arrival(slot).wait_recv()
            copy = pltpu.make_async_remote_copy(
                src_ref=x_ref if k == 0 else out_ref.at[slot],
                dst_ref=out_ref.at[slot],
                send_sem=send_sem.at[ring, k],
                recv_sem=recv_sem.at[slot],
                device_id=device_on(axis, target),
                device_id_type=MESH,
            )
            copy.start()
            copies.append(copy)
    arrival(lax.rem(me - steps[0] + n, n)).wait_recv()
    arrival(lax.rem(me + steps[1], n)).wait_recv()
    for copy in copies:
        copy.wait_send()


def ring_gather(x, axis, collective_id):
    n = lax.axis_size(axis)
    received = pl.pallas_call(
        functools.partial(ring_gather_kernel, axis, n),
        out_shape=jax.ShapeDtypeStruct((n,) + x.shape, x.dtype),
        in_specs=[pl.BlockSpec(memory_space=pl.ANY)],
        out_specs=pl.BlockSpec(memory_space=pl.ANY),
        scratch_shapes=[pltpu.SemaphoreType.DMA((2, n // 2)), pltpu.SemaphoreType.DMA((n,))],
        compiler_params=pltpu.CompilerParams(collective_id=collective_id, has_side_effects=True),
    )(x)
    whole = lax.dynamic_update_index_in_dim(received, x, lax.axis_index(axis), 0)
    return whole.reshape((n * x.shape[0],) + x.shape[1:])


def per_device(resid_in, hidden, w_down, frozen, steer, forget_flags):
    n_yh, n_z, n_c = (lax.axis_size(a) for a in DP)
    tok_rows, d_cols = resid_in.shape
    own_tokens, ff_rows = hidden.shape
    n_parts = 2
    sub = tok_rows // n_parts
    blocks = own_tokens // tok_rows
    total_tokens = own_tokens * lax.axis_size("shard")
    me_c = lax.axis_index("core")
    me_yh = lax.axis_index("yh")
    xt = hidden.reshape(blocks, n_parts, sub, ff_rows).swapaxes(0, 1)
    hp_parts, mlp_parts = [], []
    pair_w = jnp.concatenate([w_down, swap_with_partner(w_down, 9, False)], axis=0)
    for part in range(n_parts):
        if part > 0:
            xt, _ = lax.optimization_barrier((xt, reduced))
        got = gather_part(xt, part, 2 * part)
        hp = (
            got.reshape(n_yh, n_z, n_c, sub, ff_rows)
            .transpose(2, 1, 0, 3, 4)
            .reshape(n_c, n_z * n_yh * sub, ff_rows)
        )
        hp_parts.append(hp)
        from_partner = swap_with_partner(hp, 2 * part + 1, True)
        pair_rows = jnp.concatenate([hp[me_c], from_partner], axis=1)
        reduced = jnp.dot(pair_rows, pair_w, preferred_element_type=jnp.float32)
        reduced_z = lax.psum_scatter(reduced, "z", scatter_dimension=0, tiled=True)
        by_yh = reduced_z.reshape((n_yh, -1, d_cols))
        mlp_parts.append(by_yh[me_yh] + swap_with_partner(by_yh, 6 + part, True, "yh"))
    mlp_out = jnp.concatenate(mlp_parts, axis=0)
    residual = resid_in.astype(jnp.float32) + mlp_out
    updated = residual.astype(jnp.bfloat16)
    target_rows = lax.all_to_all(frozen, "shard", split_axis=1, concat_axis=0, tiled=True)
    row_block = (lax.axis_index("yh") * n_z + lax.axis_index("z")) * n_c + me_c
    start_row = row_block * tok_rows
    seq_ids = (start_row + jnp.arange(tok_rows, dtype=jnp.int32)) // SEQ_LEN
    seq_match = seq_ids[:, None] == jnp.arange(forget_flags.shape[0], dtype=jnp.int32)[None, :]
    is_forget = jnp.sum(jnp.where(seq_match, forget_flags[None, :], 0), axis=1) > 0
    target = jnp.where(
        is_forget[:, None], steer.astype(jnp.float32)[None, :], target_rows.astype(jnp.float32)
    )
    loss_weight = jnp.where(is_forget, 1.0, retain_weight).astype(jnp.float32)
    slopes = (loss_weight[:, None] * (residual - target) * (1.0 / math.sqrt(total_tokens))).astype(
        jnp.bfloat16
    )
    other_yh = swap_with_partner(slopes, 6 + n_parts, False, "yh")
    gathered = jnp.where(
        me_yh == 0,
        jnp.concatenate([slopes, other_yh], axis=0),
        jnp.concatenate([other_yh, slopes], axis=0),
    )
    gathered = ring_gather(gathered, "z", 10)
    partner_slopes = swap_with_partner(gathered, 2 * n_parts + 1, False)
    contract = (((0,), (0,)), ((), ()))
    grad_down = None
    for part in range(n_parts):
        for rows, got in ((me_c, gathered), (1 - me_c, partner_slopes)):
            s_part = got.reshape(n_z * n_yh, n_parts, sub, d_cols)[:, part].reshape(-1, d_cols)
            term = lax.dot_general(
                lax.dynamic_index_in_dim(hp_parts[part], rows, keepdims=False),
                s_part,
                contract,
                preferred_element_type=jnp.float32,
            )
            grad_down = term if grad_down is None else grad_down + term
    return (updated, grad_down)


def solution(mesh):
    n_dp, n_shard = mesh.devices.shape
    n_z = 8
    parts = mesh.devices.reshape(n_dp // (2 * n_z), n_z, 2, n_shard)
    split_mesh = Mesh(parts, DP + ("shard",))
    in_specs = (
        P(DP, "shard"),
        P("shard", DP),
        P(DP, "shard"),
        P(DP + ("shard",), None),
        P("shard"),
        P(),
    )
    out_specs = (P(DP, "shard"), P(DP, "shard"))
    return jax.shard_map(
        per_device, mesh=split_mesh, in_specs=in_specs, out_specs=out_specs, check_vma=False
    )
```

```python
import functools
import math

import jax
import jax.numpy as jnp
from jax import lax
from jax.experimental import pallas as pl
from jax.experimental.pallas import tpu as pltpu
from jax.sharding import Mesh, PartitionSpec as P

SEQ_LEN = 256
MESH = pl.DeviceIdType.MESH


retain_weight = 2.0


DP = ("yh", "z", "core")
ALL_AXES = DP + ("shard",)


def device_on(axis, index):
    return tuple(index if a == axis else lax.axis_index(a) for a in ALL_AXES)


def gather_kernel(axis, n, part, x_ref, out_ref, send_sem, recv_sem):
    me = lax.axis_index(axis)

    barrier = pltpu.get_barrier_semaphore()
    for off in range(1, n):
        peer = lax.rem(me + off, n)
        pl.semaphore_signal(barrier, inc=1, device_id=device_on(axis, peer), device_id_type=MESH)
    pl.semaphore_wait(barrier, n - 1)

    copies = []
    for off in range(1, n):
        peer = lax.rem(me + off, n)
        copy = pltpu.make_async_remote_copy(
            src_ref=x_ref.at[part],
            dst_ref=out_ref.at[me],
            send_sem=send_sem.at[off - 1],
            recv_sem=recv_sem.at[me],
            device_id=device_on(axis, peer),
            device_id_type=MESH,
        )
        copy.start()
        copies.append(copy)
    for copy in copies:
        copy.wait_send()
    for off in range(1, n):
        src = lax.rem(me + n - off, n)
        arrival = pltpu.make_async_remote_copy(
            src_ref=x_ref.at[part],
            dst_ref=out_ref.at[src],
            send_sem=send_sem.at[off - 1],
            recv_sem=recv_sem.at[src],
            device_id=device_on(axis, src),
            device_id_type=MESH,
        )
        arrival.wait_recv()


def placed_gather_kernel(n, n_zhi, part, x_ref, out_ref, send_sem, recv_sem):
    me = lax.axis_index("shard")

    def where(j):
        return out_ref.at[:, pl.ds(2 * lax.rem(j, n_zhi), 2), pl.ds(j // n_zhi, 1)]

    barrier = pltpu.get_barrier_semaphore()
    for off in range(1, n):
        peer = lax.rem(me + off, n)
        pl.semaphore_signal(barrier, inc=1, device_id=device_on("shard", peer), device_id_type=MESH)
    pl.semaphore_wait(barrier, n - 1)

    copies = []
    for off in range(1, n):
        peer = lax.rem(me + off, n)
        copy = pltpu.make_async_remote_copy(
            src_ref=x_ref.at[part],
            dst_ref=where(me),
            send_sem=send_sem.at[off - 1],
            recv_sem=recv_sem.at[me],
            device_id=device_on("shard", peer),
            device_id_type=MESH,
        )
        copy.start()
        copies.append(copy)
    for copy in copies:
        copy.wait_send()
    for off in range(1, n):
        src = lax.rem(me + n - off, n)
        arrival = pltpu.make_async_remote_copy(
            src_ref=x_ref.at[part],
            dst_ref=where(src),
            send_sem=send_sem.at[off - 1],
            recv_sem=recv_sem.at[src],
            device_id=device_on("shard", src),
            device_id_type=MESH,
        )
        arrival.wait_recv()


def gather_part(xt, part, collective_id, out_dims):
    n = lax.axis_size("shard")
    n_zhi = out_dims[1] // 2
    received = pl.pallas_call(
        functools.partial(placed_gather_kernel, n, n_zhi, part),
        out_shape=jax.ShapeDtypeStruct(out_dims, xt.dtype),
        in_specs=[pl.BlockSpec(memory_space=pl.ANY)],
        out_specs=pl.BlockSpec(memory_space=pl.ANY),
        scratch_shapes=[pltpu.SemaphoreType.DMA((n - 1,)), pltpu.SemaphoreType.DMA((n,))],
        compiler_params=pltpu.CompilerParams(collective_id=collective_id, has_side_effects=True),
        cost_estimate=pl.CostEstimate(
            flops=0, bytes_accessed=2 * n * xt[part].nbytes, transcendentals=0
        ),
    )(xt)
    me = lax.axis_index("shard")
    at = (0, 2 * lax.rem(me, n_zhi), me // n_zhi, 0, 0)
    return lax.dynamic_update_slice(received, xt[part], at)


def swap_kernel(axis, halves, x_ref, out_ref, send_sem, recv_sem):
    me = lax.axis_index(axis)
    partner = device_on(axis, 1 - me)

    barrier = pltpu.get_barrier_semaphore()
    pl.semaphore_signal(barrier, inc=1, device_id=partner, device_id_type=MESH)
    pl.semaphore_wait(barrier, 1)

    copy = pltpu.make_async_remote_copy(
        src_ref=x_ref.at[1 - me] if halves else x_ref,
        dst_ref=out_ref,
        send_sem=send_sem,
        recv_sem=recv_sem,
        device_id=partner,
        device_id_type=MESH,
    )
    copy.start()
    copy.wait()


def swap_with_partner(x, collective_id, halves, axis="core"):
    return pl.pallas_call(
        functools.partial(swap_kernel, axis, halves),
        out_shape=jax.ShapeDtypeStruct(x.shape[1:] if halves else x.shape, x.dtype),
        in_specs=[pl.BlockSpec(memory_space=pl.ANY)],
        out_specs=pl.BlockSpec(memory_space=pl.ANY),
        scratch_shapes=[pltpu.SemaphoreType.DMA(()), pltpu.SemaphoreType.DMA(())],
        compiler_params=pltpu.CompilerParams(collective_id=collective_id, has_side_effects=True),
    )(x)


def ring_gather_kernel(axis, n, x_ref, out_ref, send_sem, recv_sem):
    me = lax.axis_index(axis)
    right, left = lax.rem(me + 1, n), lax.rem(me + n - 1, n)

    barrier = pltpu.get_barrier_semaphore()
    for neighbour in (left, right):
        pl.semaphore_signal(barrier, inc=1, device_id=device_on(axis, neighbour), device_id_type=MESH)
    pl.semaphore_wait(barrier, 2)

    def arrival(slot):
        return pltpu.make_async_remote_copy(
            src_ref=x_ref,
            dst_ref=out_ref.at[slot],
            send_sem=send_sem.at[0, 0],
            recv_sem=recv_sem.at[slot],
            device_id=device_on(axis, left),
            device_id_type=MESH,
        )

    copies = []
    steps = (n // 2, (n - 1) // 2)
    for k in range(max(steps)):
        for ring, (sign, target) in enumerate(((-1, right), (1, left))):
            if k >= steps[ring]:
                continue
            slot = lax.rem(me + sign * k + n, n)
            if k > 0:
                arrival(slot).wait_recv()
            copy = pltpu.make_async_remote_copy(
                src_ref=x_ref if k == 0 else out_ref.at[slot],
                dst_ref=out_ref.at[slot],
                send_sem=send_sem.at[ring, k],
                recv_sem=recv_sem.at[slot],
                device_id=device_on(axis, target),
                device_id_type=MESH,
            )
            copy.start()
            copies.append(copy)
    arrival(lax.rem(me - steps[0] + n, n)).wait_recv()
    arrival(lax.rem(me + steps[1], n)).wait_recv()
    for copy in copies:
        copy.wait_send()


def ring_gather(x, axis, collective_id):
    n = lax.axis_size(axis)
    received = pl.pallas_call(
        functools.partial(ring_gather_kernel, axis, n),
        out_shape=jax.ShapeDtypeStruct((n,) + x.shape, x.dtype),
        in_specs=[pl.BlockSpec(memory_space=pl.ANY)],
        out_specs=pl.BlockSpec(memory_space=pl.ANY),
        scratch_shapes=[pltpu.SemaphoreType.DMA((2, n // 2)), pltpu.SemaphoreType.DMA((n,))],
        compiler_params=pltpu.CompilerParams(collective_id=collective_id, has_side_effects=True),
    )(x)
    whole = lax.dynamic_update_index_in_dim(received, x, lax.axis_index(axis), 0)
    return whole.reshape((n * x.shape[0],) + x.shape[1:])


def per_device(resid_in, hidden, w_down, frozen, steer, forget_flags):
    n_yh, n_z, n_c = (lax.axis_size(a) for a in DP)
    tok_rows, d_cols = resid_in.shape
    own_tokens, ff_rows = hidden.shape
    n_parts = 2
    sub = tok_rows // n_parts
    blocks = own_tokens // tok_rows
    total_tokens = own_tokens * lax.axis_size("shard")
    me_c = lax.axis_index("core")
    me_yh = lax.axis_index("yh")
    xt = hidden.reshape(blocks // n_c, n_c, n_parts, 1, sub, ff_rows).transpose(2, 1, 0, 3, 4, 5)
    hp_parts, mlp_parts = [], []
    pair_w = jnp.concatenate([w_down, swap_with_partner(w_down, 9, False)], axis=0)
    for part in range(n_parts):
        if part > 0:
            xt, _ = lax.optimization_barrier((xt, reduced))
        got = gather_part(xt, part, 2 * part, (n_c, n_z, n_yh, sub, ff_rows))
        hp = got.reshape(n_c, n_z * n_yh * sub, ff_rows)
        hp_parts.append(hp)
        from_partner = swap_with_partner(hp, 2 * part + 1, True)
        pair_rows = jnp.concatenate([hp[me_c], from_partner], axis=1)
        reduced = jnp.dot(pair_rows, pair_w, preferred_element_type=jnp.float32)
        reduced_z = lax.psum_scatter(reduced, "z", scatter_dimension=0, tiled=True)
        by_yh = reduced_z.reshape((n_yh, -1, d_cols))
        mlp_parts.append(by_yh[me_yh] + swap_with_partner(by_yh, 6 + part, True, "yh"))
    mlp_out = jnp.concatenate(mlp_parts, axis=0)
    residual = resid_in.astype(jnp.float32) + mlp_out
    updated = residual.astype(jnp.bfloat16)
    target_rows = lax.all_to_all(frozen, "shard", split_axis=1, concat_axis=0, tiled=True)
    row_block = (lax.axis_index("yh") * n_z + lax.axis_index("z")) * n_c + me_c
    start_row = row_block * tok_rows
    seq_ids = (start_row + jnp.arange(tok_rows, dtype=jnp.int32)) // SEQ_LEN
    seq_match = seq_ids[:, None] == jnp.arange(forget_flags.shape[0], dtype=jnp.int32)[None, :]
    is_forget = jnp.sum(jnp.where(seq_match, forget_flags[None, :], 0), axis=1) > 0
    target = jnp.where(
        is_forget[:, None], steer.astype(jnp.float32)[None, :], target_rows.astype(jnp.float32)
    )
    loss_weight = jnp.where(is_forget, 1.0, retain_weight).astype(jnp.float32)
    slopes = (loss_weight[:, None] * (residual - target) * (1.0 / math.sqrt(total_tokens))).astype(
        jnp.bfloat16
    )
    other_yh = swap_with_partner(slopes, 6 + n_parts, False, "yh")
    gathered = jnp.where(
        me_yh == 0,
        jnp.concatenate([slopes, other_yh], axis=0),
        jnp.concatenate([other_yh, slopes], axis=0),
    )
    gathered = ring_gather(gathered, "z", 10)
    partner_slopes = swap_with_partner(gathered, 2 * n_parts + 1, False)
    contract = (((0,), (0,)), ((), ()))
    grad_down = None
    for part in range(n_parts):
        for rows, got in ((me_c, gathered), (1 - me_c, partner_slopes)):
            s_part = got.reshape(n_z * n_yh, n_parts, sub, d_cols)[:, part].reshape(-1, d_cols)
            term = lax.dot_general(
                lax.dynamic_index_in_dim(hp_parts[part], rows, keepdims=False),
                s_part,
                contract,
                preferred_element_type=jnp.float32,
            )
            grad_down = term if grad_down is None else grad_down + term
    return (updated, grad_down)


def solution(mesh):
    n_dp, n_shard = mesh.devices.shape
    n_z = 8
    parts = mesh.devices.reshape(n_dp // (2 * n_z), n_z, 2, n_shard)
    split_mesh = Mesh(parts, DP + ("shard",))
    in_specs = (
        P(DP, "shard"),
        P("shard", DP),
        P(DP, "shard"),
        P(DP + ("shard",), None),
        P("shard"),
        P(),
    )
    out_specs = (P(DP, "shard"), P(DP, "shard"))
    return jax.shard_map(
        per_device, mesh=split_mesh, in_specs=in_specs, out_specs=out_specs, check_vma=False
    )
```

```python
import functools
import math

import jax
import jax.numpy as jnp
from jax import lax
from jax.experimental import pallas as pl
from jax.experimental.pallas import tpu as pltpu
from jax.sharding import Mesh, PartitionSpec as P

SEQ_LEN = 256
MESH = pl.DeviceIdType.MESH


retain_weight = 2.0


DP = ("yh", "z", "core")
ALL_AXES = DP + ("shard",)


def device_on(axis, index):
    return tuple(index if a == axis else lax.axis_index(a) for a in ALL_AXES)


def gather_kernel(axis, n, part, x_ref, out_ref, send_sem, recv_sem):
    me = lax.axis_index(axis)

    barrier = pltpu.get_barrier_semaphore()
    for off in range(1, n):
        peer = lax.rem(me + off, n)
        pl.semaphore_signal(barrier, inc=1, device_id=device_on(axis, peer), device_id_type=MESH)
    pl.semaphore_wait(barrier, n - 1)

    copies = []
    for off in range(1, n):
        peer = lax.rem(me + off, n)
        copy = pltpu.make_async_remote_copy(
            src_ref=x_ref.at[part],
            dst_ref=out_ref.at[me],
            send_sem=send_sem.at[off - 1],
            recv_sem=recv_sem.at[me],
            device_id=device_on(axis, peer),
            device_id_type=MESH,
        )
        copy.start()
        copies.append(copy)
    for copy in copies:
        copy.wait_send()
    for off in range(1, n):
        src = lax.rem(me + n - off, n)
        arrival = pltpu.make_async_remote_copy(
            src_ref=x_ref.at[part],
            dst_ref=out_ref.at[src],
            send_sem=send_sem.at[off - 1],
            recv_sem=recv_sem.at[src],
            device_id=device_on(axis, src),
            device_id_type=MESH,
        )
        arrival.wait_recv()


def placed_gather_kernel(n, n_zhi, part, x_ref, out_ref, send_sem, recv_sem):
    me = lax.axis_index("shard")

    def where(j):
        return out_ref.at[:, pl.ds(2 * lax.rem(j, n_zhi), 2), pl.ds(j // n_zhi, 1)]

    barrier = pltpu.get_barrier_semaphore()
    for off in range(1, n):
        peer = lax.rem(me + off, n)
        pl.semaphore_signal(barrier, inc=1, device_id=device_on("shard", peer), device_id_type=MESH)
    pl.semaphore_wait(barrier, n - 1)

    copies = []
    for off in range(1, n):
        peer = lax.rem(me + off, n)
        copy = pltpu.make_async_remote_copy(
            src_ref=x_ref.at[part],
            dst_ref=where(me),
            send_sem=send_sem.at[off - 1],
            recv_sem=recv_sem.at[me],
            device_id=device_on("shard", peer),
            device_id_type=MESH,
        )
        copy.start()
        copies.append(copy)
    for copy in copies:
        copy.wait_send()
    for off in range(1, n):
        src = lax.rem(me + n - off, n)
        arrival = pltpu.make_async_remote_copy(
            src_ref=x_ref.at[part],
            dst_ref=where(src),
            send_sem=send_sem.at[off - 1],
            recv_sem=recv_sem.at[src],
            device_id=device_on("shard", src),
            device_id_type=MESH,
        )
        arrival.wait_recv()


def gather_part(xt, part, collective_id, out_dims):
    n = lax.axis_size("shard")
    n_zhi = out_dims[1] // 2
    received = pl.pallas_call(
        functools.partial(placed_gather_kernel, n, n_zhi, part),
        out_shape=jax.ShapeDtypeStruct(out_dims, xt.dtype),
        in_specs=[pl.BlockSpec(memory_space=pl.ANY)],
        out_specs=pl.BlockSpec(memory_space=pl.ANY),
        scratch_shapes=[pltpu.SemaphoreType.DMA((n - 1,)), pltpu.SemaphoreType.DMA((n,))],
        compiler_params=pltpu.CompilerParams(collective_id=collective_id, has_side_effects=True),
        cost_estimate=pl.CostEstimate(
            flops=0, bytes_accessed=2 * n * xt[part].nbytes, transcendentals=0
        ),
    )(xt)
    me = lax.axis_index("shard")
    at = (0, 2 * lax.rem(me, n_zhi), me // n_zhi, 0, 0)
    return lax.dynamic_update_slice(received, xt[part], at)


def swap_kernel(axis, halves, x_ref, out_ref, send_sem, recv_sem):
    me = lax.axis_index(axis)
    partner = device_on(axis, 1 - me)

    barrier = pltpu.get_barrier_semaphore()
    pl.semaphore_signal(barrier, inc=1, device_id=partner, device_id_type=MESH)
    pl.semaphore_wait(barrier, 1)

    copy = pltpu.make_async_remote_copy(
        src_ref=x_ref.at[1 - me] if halves else x_ref,
        dst_ref=out_ref,
        send_sem=send_sem,
        recv_sem=recv_sem,
        device_id=partner,
        device_id_type=MESH,
    )
    copy.start()
    copy.wait()


def swap_with_partner(x, collective_id, halves, axis="core"):
    return pl.pallas_call(
        functools.partial(swap_kernel, axis, halves),
        out_shape=jax.ShapeDtypeStruct(x.shape[1:] if halves else x.shape, x.dtype),
        in_specs=[pl.BlockSpec(memory_space=pl.ANY)],
        out_specs=pl.BlockSpec(memory_space=pl.ANY),
        scratch_shapes=[pltpu.SemaphoreType.DMA(()), pltpu.SemaphoreType.DMA(())],
        compiler_params=pltpu.CompilerParams(collective_id=collective_id, has_side_effects=True),
    )(x)


def ring_gather_kernel(axis, n, x_ref, out_ref, send_sem, recv_sem):
    me = lax.axis_index(axis)
    right, left = lax.rem(me + 1, n), lax.rem(me + n - 1, n)

    barrier = pltpu.get_barrier_semaphore()
    for neighbour in (left, right):
        pl.semaphore_signal(barrier, inc=1, device_id=device_on(axis, neighbour), device_id_type=MESH)
    pl.semaphore_wait(barrier, 2)

    def arrival(slot):
        return pltpu.make_async_remote_copy(
            src_ref=x_ref,
            dst_ref=out_ref.at[slot],
            send_sem=send_sem.at[0, 0],
            recv_sem=recv_sem.at[slot],
            device_id=device_on(axis, left),
            device_id_type=MESH,
        )

    copies = []
    steps = (n // 2, (n - 1) // 2)
    for k in range(max(steps)):
        for ring, (sign, target) in enumerate(((-1, right), (1, left))):
            if k >= steps[ring]:
                continue
            slot = lax.rem(me + sign * k + n, n)
            if k > 0:
                arrival(slot).wait_recv()
            copy = pltpu.make_async_remote_copy(
                src_ref=x_ref if k == 0 else out_ref.at[slot],
                dst_ref=out_ref.at[slot],
                send_sem=send_sem.at[ring, k],
                recv_sem=recv_sem.at[slot],
                device_id=device_on(axis, target),
                device_id_type=MESH,
            )
            copy.start()
            copies.append(copy)
    arrival(lax.rem(me - steps[0] + n, n)).wait_recv()
    arrival(lax.rem(me + steps[1], n)).wait_recv()
    for copy in copies:
        copy.wait_send()


def ring_gather(x, axis, collective_id):
    n = lax.axis_size(axis)
    received = pl.pallas_call(
        functools.partial(ring_gather_kernel, axis, n),
        out_shape=jax.ShapeDtypeStruct((n,) + x.shape, x.dtype),
        in_specs=[pl.BlockSpec(memory_space=pl.ANY)],
        out_specs=pl.BlockSpec(memory_space=pl.ANY),
        scratch_shapes=[pltpu.SemaphoreType.DMA((2, n // 2)), pltpu.SemaphoreType.DMA((n,))],
        compiler_params=pltpu.CompilerParams(collective_id=collective_id, has_side_effects=True),
    )(x)
    whole = lax.dynamic_update_index_in_dim(received, x, lax.axis_index(axis), 0)
    return whole.reshape((n * x.shape[0],) + x.shape[1:])


def ring_scatter_kernel(axis, n, x_ref, out_ref, recv, send, send_sem, recv_sem, credit):
    me = lax.axis_index(axis)
    right, left = lax.rem(me + 1, n), lax.rem(me + n - 1, n)
    half = out_ref.shape[1] // 2

    barrier = pltpu.get_barrier_semaphore()
    for neighbour in (left, right):
        pl.semaphore_signal(barrier, inc=1, device_id=device_on(axis, neighbour), device_id_type=MESH)
    pl.semaphore_wait(barrier, 2)

    rings = ((1, right, left), (-1, left, right))

    def transfer(ring, slot, target):
        return pltpu.make_async_remote_copy(
            src_ref=send.at[ring, slot],
            dst_ref=recv.at[ring, slot],
            send_sem=send_sem.at[ring, slot],
            recv_sem=recv_sem.at[ring, slot],
            device_id=device_on(axis, target),
            device_id_type=MESH,
        )

    pending = {}
    for k in range(n - 1):
        slot = k % 2
        for ring, (sign, target, source) in enumerate(rings):
            cols = pl.ds(ring * half, half)
            dest = lax.rem(me - sign * (k + 1) + 2 * n, n)
            if k >= 2:
                pending[ring, slot].wait_send()
                pl.semaphore_wait(credit.at[ring], 1)
            own = x_ref[dest, :, cols]
            if k == 0:
                send[ring, slot] = own
            else:
                transfer(ring, 1 - slot, target).wait_recv()
                send[ring, slot] = recv[ring, 1 - slot] + own
                if k < n - 2:
                    pl.semaphore_signal(credit.at[ring], inc=1, device_id=device_on(axis, source), device_id_type=MESH)
            copy = transfer(ring, slot, target)
            copy.start()
            pending[ring, slot] = copy
    last = (n - 2) % 2
    for ring, (sign, target, source) in enumerate(rings):
        cols = pl.ds(ring * half, half)
        transfer(ring, last, target).wait_recv()
        out_ref[:, cols] = recv[ring, last] + x_ref[me, :, cols]
    for copy in pending.values():
        copy.wait_send()


def ring_scatter(x, axis, collective_id):
    n = x.shape[0]
    rows, cols = x.shape[1:]
    return pl.pallas_call(
        functools.partial(ring_scatter_kernel, axis, n),
        out_shape=jax.ShapeDtypeStruct((rows, cols), x.dtype),
        in_specs=[pl.BlockSpec(memory_space=pltpu.VMEM)],
        out_specs=pl.BlockSpec(memory_space=pltpu.VMEM),
        scratch_shapes=[
            pltpu.VMEM((2, 2, rows, cols // 2), x.dtype),
            pltpu.VMEM((2, 2, rows, cols // 2), x.dtype),
            pltpu.SemaphoreType.DMA((2, 2)),
            pltpu.SemaphoreType.DMA((2, 2)),
            pltpu.SemaphoreType.REGULAR((2,)),
        ],
        compiler_params=pltpu.CompilerParams(
            collective_id=collective_id, has_side_effects=True, vmem_limit_bytes=48 * 1024 * 1024
        ),
    )(x)


def per_device(resid_in, hidden, w_down, frozen, steer, forget_flags):
    n_yh, n_z, n_c = (lax.axis_size(a) for a in DP)
    tok_rows, d_cols = resid_in.shape
    own_tokens, ff_rows = hidden.shape
    n_parts = 2
    sub = tok_rows // n_parts
    blocks = own_tokens // tok_rows
    total_tokens = own_tokens * lax.axis_size("shard")
    me_c = lax.axis_index("core")
    me_yh = lax.axis_index("yh")
    xt = hidden.reshape(blocks // n_c, n_c, n_parts, 1, sub, ff_rows).transpose(2, 1, 0, 3, 4, 5)
    hp_parts, mlp_parts = [], []
    pair_w = jnp.concatenate([w_down, swap_with_partner(w_down, 9, False)], axis=0)
    for part in range(n_parts):
        if part > 0:
            xt, _ = lax.optimization_barrier((xt, reduced))
        got = gather_part(xt, part, 2 * part, (n_c, n_z, n_yh, sub, ff_rows))
        hp = got.reshape(n_c, n_z * n_yh * sub, ff_rows)
        hp_parts.append(hp)
        from_partner = swap_with_partner(hp, 2 * part + 1, True)
        pair_rows = jnp.concatenate([hp[me_c], from_partner], axis=1)
        reduced = jnp.dot(pair_rows, pair_w, preferred_element_type=jnp.float32)
        if part == 0:
            reduced_z = lax.psum_scatter(reduced, "z", scatter_dimension=0, tiled=True)
        else:
            reduced_z = ring_scatter(reduced.reshape((n_z, -1, d_cols)), "z", 11)
        by_yh = reduced_z.reshape((n_yh, -1, d_cols))
        mlp_parts.append(by_yh[me_yh] + swap_with_partner(by_yh, 6 + part, True, "yh"))
    mlp_out = jnp.concatenate(mlp_parts, axis=0)
    residual = resid_in.astype(jnp.float32) + mlp_out
    updated = residual.astype(jnp.bfloat16)
    target_rows = lax.all_to_all(frozen, "shard", split_axis=1, concat_axis=0, tiled=True)
    row_block = (lax.axis_index("yh") * n_z + lax.axis_index("z")) * n_c + me_c
    start_row = row_block * tok_rows
    seq_ids = (start_row + jnp.arange(tok_rows, dtype=jnp.int32)) // SEQ_LEN
    seq_match = seq_ids[:, None] == jnp.arange(forget_flags.shape[0], dtype=jnp.int32)[None, :]
    is_forget = jnp.sum(jnp.where(seq_match, forget_flags[None, :], 0), axis=1) > 0
    target = jnp.where(
        is_forget[:, None], steer.astype(jnp.float32)[None, :], target_rows.astype(jnp.float32)
    )
    loss_weight = jnp.where(is_forget, 1.0, retain_weight).astype(jnp.float32)
    slopes = (loss_weight[:, None] * (residual - target) * (1.0 / math.sqrt(total_tokens))).astype(
        jnp.bfloat16
    )
    other_yh = swap_with_partner(slopes, 6 + n_parts, False, "yh")
    gathered = jnp.where(
        me_yh == 0,
        jnp.concatenate([slopes, other_yh], axis=0),
        jnp.concatenate([other_yh, slopes], axis=0),
    )
    gathered = ring_gather(gathered, "z", 10)
    partner_slopes = swap_with_partner(gathered, 2 * n_parts + 1, False)
    contract = (((0,), (0,)), ((), ()))
    grad_down = None
    for part in range(n_parts):
        for rows, got in ((me_c, gathered), (1 - me_c, partner_slopes)):
            s_part = got.reshape(n_z * n_yh, n_parts, sub, d_cols)[:, part].reshape(-1, d_cols)
            term = lax.dot_general(
                lax.dynamic_index_in_dim(hp_parts[part], rows, keepdims=False),
                s_part,
                contract,
                preferred_element_type=jnp.float32,
            )
            grad_down = term if grad_down is None else grad_down + term
    return (updated, grad_down)


def solution(mesh):
    n_dp, n_shard = mesh.devices.shape
    n_z = 8
    parts = mesh.devices.reshape(n_dp // (2 * n_z), n_z, 2, n_shard)
    split_mesh = Mesh(parts, DP + ("shard",))
    in_specs = (
        P(DP, "shard"),
        P("shard", DP),
        P(DP, "shard"),
        P(DP + ("shard",), None),
        P("shard"),
        P(),
    )
    out_specs = (P(DP, "shard"), P(DP, "shard"))
    return jax.shard_map(
        per_device, mesh=split_mesh, in_specs=in_specs, out_specs=out_specs, check_vma=False
    )
```

```python
import functools
import math

import jax
import jax.numpy as jnp
from jax import lax
from jax.experimental import pallas as pl
from jax.experimental.pallas import tpu as pltpu
from jax.sharding import Mesh, PartitionSpec as P

SEQ_LEN = 256
MESH = pl.DeviceIdType.MESH


retain_weight = 2.0


DP = ("yh", "z", "core")
ALL_AXES = DP + ("shard",)


def device_on(axis, index):
    return tuple(index if a == axis else lax.axis_index(a) for a in ALL_AXES)


def gather_kernel(axis, n, part, x_ref, out_ref, send_sem, recv_sem):
    me = lax.axis_index(axis)

    barrier = pltpu.get_barrier_semaphore()
    for off in range(1, n):
        peer = lax.rem(me + off, n)
        pl.semaphore_signal(barrier, inc=1, device_id=device_on(axis, peer), device_id_type=MESH)
    pl.semaphore_wait(barrier, n - 1)

    copies = []
    for off in range(1, n):
        peer = lax.rem(me + off, n)
        copy = pltpu.make_async_remote_copy(
            src_ref=x_ref.at[part],
            dst_ref=out_ref.at[me],
            send_sem=send_sem.at[off - 1],
            recv_sem=recv_sem.at[me],
            device_id=device_on(axis, peer),
            device_id_type=MESH,
        )
        copy.start()
        copies.append(copy)
    for copy in copies:
        copy.wait_send()
    for off in range(1, n):
        src = lax.rem(me + n - off, n)
        arrival = pltpu.make_async_remote_copy(
            src_ref=x_ref.at[part],
            dst_ref=out_ref.at[src],
            send_sem=send_sem.at[off - 1],
            recv_sem=recv_sem.at[src],
            device_id=device_on(axis, src),
            device_id_type=MESH,
        )
        arrival.wait_recv()


def placed_gather_kernel(n, n_zhi, part, x_ref, out_ref, send_sem, recv_sem):
    me = lax.axis_index("shard")

    def where(j):
        return out_ref.at[:, pl.ds(2 * lax.rem(j, n_zhi), 2), pl.ds(j // n_zhi, 1)]

    barrier = pltpu.get_barrier_semaphore()
    for off in range(1, n):
        peer = lax.rem(me + off, n)
        pl.semaphore_signal(barrier, inc=1, device_id=device_on("shard", peer), device_id_type=MESH)
    pl.semaphore_wait(barrier, n - 1)

    copies = []
    for off in range(1, n):
        peer = lax.rem(me + off, n)
        copy = pltpu.make_async_remote_copy(
            src_ref=x_ref.at[part],
            dst_ref=where(me),
            send_sem=send_sem.at[off - 1],
            recv_sem=recv_sem.at[me],
            device_id=device_on("shard", peer),
            device_id_type=MESH,
        )
        copy.start()
        copies.append(copy)
    for copy in copies:
        copy.wait_send()
    for off in range(1, n):
        src = lax.rem(me + n - off, n)
        arrival = pltpu.make_async_remote_copy(
            src_ref=x_ref.at[part],
            dst_ref=where(src),
            send_sem=send_sem.at[off - 1],
            recv_sem=recv_sem.at[src],
            device_id=device_on("shard", src),
            device_id_type=MESH,
        )
        arrival.wait_recv()


def gather_part(xt, part, collective_id, out_dims):
    n = lax.axis_size("shard")
    n_zhi = out_dims[1] // 2
    received = pl.pallas_call(
        functools.partial(placed_gather_kernel, n, n_zhi, part),
        out_shape=jax.ShapeDtypeStruct(out_dims, xt.dtype),
        in_specs=[pl.BlockSpec(memory_space=pl.ANY)],
        out_specs=pl.BlockSpec(memory_space=pl.ANY),
        scratch_shapes=[pltpu.SemaphoreType.DMA((n - 1,)), pltpu.SemaphoreType.DMA((n,))],
        compiler_params=pltpu.CompilerParams(collective_id=collective_id, has_side_effects=True),
        cost_estimate=pl.CostEstimate(
            flops=0, bytes_accessed=2 * n * xt[part].nbytes, transcendentals=0
        ),
    )(xt)
    me = lax.axis_index("shard")
    at = (0, 2 * lax.rem(me, n_zhi), me // n_zhi, 0, 0)
    return lax.dynamic_update_slice(received, xt[part], at)


def swap_kernel(axis, halves, x_ref, out_ref, send_sem, recv_sem):
    me = lax.axis_index(axis)
    partner = device_on(axis, 1 - me)

    barrier = pltpu.get_barrier_semaphore()
    pl.semaphore_signal(barrier, inc=1, device_id=partner, device_id_type=MESH)
    pl.semaphore_wait(barrier, 1)

    copy = pltpu.make_async_remote_copy(
        src_ref=x_ref.at[1 - me] if halves else x_ref,
        dst_ref=out_ref,
        send_sem=send_sem,
        recv_sem=recv_sem,
        device_id=partner,
        device_id_type=MESH,
    )
    copy.start()
    copy.wait()


def swap_with_partner(x, collective_id, halves, axis="core"):
    return pl.pallas_call(
        functools.partial(swap_kernel, axis, halves),
        out_shape=jax.ShapeDtypeStruct(x.shape[1:] if halves else x.shape, x.dtype),
        in_specs=[pl.BlockSpec(memory_space=pl.ANY)],
        out_specs=pl.BlockSpec(memory_space=pl.ANY),
        scratch_shapes=[pltpu.SemaphoreType.DMA(()), pltpu.SemaphoreType.DMA(())],
        compiler_params=pltpu.CompilerParams(collective_id=collective_id, has_side_effects=True),
    )(x)


def ring_gather_kernel(axis, n, x_ref, out_ref, send_sem, recv_sem):
    me = lax.axis_index(axis)
    right, left = lax.rem(me + 1, n), lax.rem(me + n - 1, n)

    barrier = pltpu.get_barrier_semaphore()
    for neighbour in (left, right):
        pl.semaphore_signal(barrier, inc=1, device_id=device_on(axis, neighbour), device_id_type=MESH)
    pl.semaphore_wait(barrier, 2)

    def arrival(slot):
        return pltpu.make_async_remote_copy(
            src_ref=x_ref,
            dst_ref=out_ref.at[slot],
            send_sem=send_sem.at[0, 0],
            recv_sem=recv_sem.at[slot],
            device_id=device_on(axis, left),
            device_id_type=MESH,
        )

    copies = []
    steps = (n // 2, (n - 1) // 2)
    for k in range(max(steps)):
        for ring, (sign, target) in enumerate(((-1, right), (1, left))):
            if k >= steps[ring]:
                continue
            slot = lax.rem(me + sign * k + n, n)
            if k > 0:
                arrival(slot).wait_recv()
            copy = pltpu.make_async_remote_copy(
                src_ref=x_ref if k == 0 else out_ref.at[slot],
                dst_ref=out_ref.at[slot],
                send_sem=send_sem.at[ring, k],
                recv_sem=recv_sem.at[slot],
                device_id=device_on(axis, target),
                device_id_type=MESH,
            )
            copy.start()
            copies.append(copy)
    arrival(lax.rem(me - steps[0] + n, n)).wait_recv()
    arrival(lax.rem(me + steps[1], n)).wait_recv()
    for copy in copies:
        copy.wait_send()


def ring_gather(x, axis, collective_id):
    n = lax.axis_size(axis)
    received = pl.pallas_call(
        functools.partial(ring_gather_kernel, axis, n),
        out_shape=jax.ShapeDtypeStruct((n,) + x.shape, x.dtype),
        in_specs=[pl.BlockSpec(memory_space=pl.ANY)],
        out_specs=pl.BlockSpec(memory_space=pl.ANY),
        scratch_shapes=[pltpu.SemaphoreType.DMA((2, n // 2)), pltpu.SemaphoreType.DMA((n,))],
        compiler_params=pltpu.CompilerParams(collective_id=collective_id, has_side_effects=True),
    )(x)
    whole = lax.dynamic_update_index_in_dim(received, x, lax.axis_index(axis), 0)
    return whole.reshape((n * x.shape[0],) + x.shape[1:])


def ring_scatter_kernel(axis, n, x_ref, out_ref, recv, send, send_sem, recv_sem, credit):
    me = lax.axis_index(axis)
    right, left = lax.rem(me + 1, n), lax.rem(me + n - 1, n)
    half = out_ref.shape[1] // 2

    barrier = pltpu.get_barrier_semaphore()
    for neighbour in (left, right):
        pl.semaphore_signal(barrier, inc=1, device_id=device_on(axis, neighbour), device_id_type=MESH)
    pl.semaphore_wait(barrier, 2)

    rings = ((1, right, left), (-1, left, right))

    def transfer(ring, slot, target):
        return pltpu.make_async_remote_copy(
            src_ref=send.at[ring, slot],
            dst_ref=recv.at[ring, slot],
            send_sem=send_sem.at[ring, slot],
            recv_sem=recv_sem.at[ring, slot],
            device_id=device_on(axis, target),
            device_id_type=MESH,
        )

    pending = {}
    for k in range(n - 1):
        slot = k % 2
        for ring, (sign, target, source) in enumerate(rings):
            cols = pl.ds(ring * half, half)
            dest = lax.rem(me - sign * (k + 1) + 2 * n, n)
            if k >= 2:
                pending[ring, slot].wait_send()
                pl.semaphore_wait(credit.at[ring], 1)
            own = x_ref[dest, :, cols]
            if k == 0:
                send[ring, slot] = own
            else:
                transfer(ring, 1 - slot, target).wait_recv()
                send[ring, slot] = recv[ring, 1 - slot] + own
                if k < n - 2:
                    pl.semaphore_signal(credit.at[ring], inc=1, device_id=device_on(axis, source), device_id_type=MESH)
            copy = transfer(ring, slot, target)
            copy.start()
            pending[ring, slot] = copy
    last = (n - 2) % 2
    for ring, (sign, target, source) in enumerate(rings):
        cols = pl.ds(ring * half, half)
        transfer(ring, last, target).wait_recv()
        out_ref[:, cols] = recv[ring, last] + x_ref[me, :, cols]
    for copy in pending.values():
        copy.wait_send()


def ring_scatter(x, axis, collective_id):
    n = x.shape[0]
    rows, cols = x.shape[1:]
    return pl.pallas_call(
        functools.partial(ring_scatter_kernel, axis, n),
        out_shape=jax.ShapeDtypeStruct((rows, cols), x.dtype),
        in_specs=[pl.BlockSpec(memory_space=pltpu.VMEM)],
        out_specs=pl.BlockSpec(memory_space=pltpu.VMEM),
        scratch_shapes=[
            pltpu.VMEM((2, 2, rows, cols // 2), x.dtype),
            pltpu.VMEM((2, 2, rows, cols // 2), x.dtype),
            pltpu.SemaphoreType.DMA((2, 2)),
            pltpu.SemaphoreType.DMA((2, 2)),
            pltpu.SemaphoreType.REGULAR((2,)),
        ],
        compiler_params=pltpu.CompilerParams(
            collective_id=collective_id, has_side_effects=True, vmem_limit_bytes=48 * 1024 * 1024
        ),
    )(x)


def per_device(resid_in, hidden, w_down, frozen, steer, forget_flags):
    n_yh, n_z, n_c = (lax.axis_size(a) for a in DP)
    tok_rows, d_cols = resid_in.shape
    own_tokens, ff_rows = hidden.shape
    n_parts = 2
    sub = tok_rows // n_parts
    blocks = own_tokens // tok_rows
    total_tokens = own_tokens * lax.axis_size("shard")
    me_c = lax.axis_index("core")
    me_yh = lax.axis_index("yh")
    xt = hidden.reshape(blocks // n_c, n_c, n_parts, 1, sub, ff_rows).transpose(2, 1, 0, 3, 4, 5)
    hp_parts, mlp_parts = [], []
    pair_w = jnp.concatenate([w_down, swap_with_partner(w_down, 9, False)], axis=0)
    for part in range(n_parts):
        if part > 0:
            xt, _ = lax.optimization_barrier((xt, reduced))
        got = gather_part(xt, part, 2 * part, (n_c, n_z, n_yh, sub, ff_rows))
        hp = got.reshape(n_c, n_z * n_yh * sub, ff_rows)
        hp_parts.append(hp)
        from_partner = swap_with_partner(hp, 2 * part + 1, True)
        pair_rows = jnp.concatenate([hp[me_c], from_partner], axis=1)
        reduced = jnp.dot(pair_rows, pair_w, preferred_element_type=jnp.float32)
        if part == 0:
            reduced_z = first_z = lax.psum_scatter(reduced, "z", scatter_dimension=0, tiled=True)
        else:
            split = d_cols // 2
            sc_cols, _ = lax.optimization_barrier((reduced[:, :split], first_z))
            on_sc = lax.psum_scatter(sc_cols, "z", scatter_dimension=0, tiled=True)
            on_tc = ring_scatter(reduced[:, split:].reshape((n_z, -1, d_cols - split)), "z", 11)
            reduced_z = jnp.concatenate([on_sc, on_tc], axis=1)
        by_yh = reduced_z.reshape((n_yh, -1, d_cols))
        mlp_parts.append(by_yh[me_yh] + swap_with_partner(by_yh, 6 + part, True, "yh"))
    mlp_out = jnp.concatenate(mlp_parts, axis=0)
    residual = resid_in.astype(jnp.float32) + mlp_out
    updated = residual.astype(jnp.bfloat16)
    target_rows = lax.all_to_all(frozen, "shard", split_axis=1, concat_axis=0, tiled=True)
    row_block = (lax.axis_index("yh") * n_z + lax.axis_index("z")) * n_c + me_c
    start_row = row_block * tok_rows
    seq_ids = (start_row + jnp.arange(tok_rows, dtype=jnp.int32)) // SEQ_LEN
    seq_match = seq_ids[:, None] == jnp.arange(forget_flags.shape[0], dtype=jnp.int32)[None, :]
    is_forget = jnp.sum(jnp.where(seq_match, forget_flags[None, :], 0), axis=1) > 0
    target = jnp.where(
        is_forget[:, None], steer.astype(jnp.float32)[None, :], target_rows.astype(jnp.float32)
    )
    loss_weight = jnp.where(is_forget, 1.0, retain_weight).astype(jnp.float32)
    slopes = (loss_weight[:, None] * (residual - target) * (1.0 / math.sqrt(total_tokens))).astype(
        jnp.bfloat16
    )
    other_yh = swap_with_partner(slopes, 6 + n_parts, False, "yh")
    gathered = jnp.where(
        me_yh == 0,
        jnp.concatenate([slopes, other_yh], axis=0),
        jnp.concatenate([other_yh, slopes], axis=0),
    )
    gathered = ring_gather(gathered, "z", 10)
    partner_slopes = swap_with_partner(gathered, 2 * n_parts + 1, False)
    contract = (((0,), (0,)), ((), ()))
    grad_down = None
    for part in range(n_parts):
        for rows, got in ((me_c, gathered), (1 - me_c, partner_slopes)):
            s_part = got.reshape(n_z * n_yh, n_parts, sub, d_cols)[:, part].reshape(-1, d_cols)
            term = lax.dot_general(
                lax.dynamic_index_in_dim(hp_parts[part], rows, keepdims=False),
                s_part,
                contract,
                preferred_element_type=jnp.float32,
            )
            grad_down = term if grad_down is None else grad_down + term
    return (updated, grad_down)


def solution(mesh):
    n_dp, n_shard = mesh.devices.shape
    n_z = 8
    parts = mesh.devices.reshape(n_dp // (2 * n_z), n_z, 2, n_shard)
    split_mesh = Mesh(parts, DP + ("shard",))
    in_specs = (
        P(DP, "shard"),
        P("shard", DP),
        P(DP, "shard"),
        P(DP + ("shard",), None),
        P("shard"),
        P(),
    )
    out_specs = (P(DP, "shard"), P(DP, "shard"))
    return jax.shard_map(
        per_device, mesh=split_mesh, in_specs=in_specs, out_specs=out_specs, check_vma=False
    )
```

```python
import functools
import math

import jax
import jax.numpy as jnp
from jax import lax
from jax.experimental import pallas as pl
from jax.experimental.pallas import tpu as pltpu
from jax.sharding import Mesh, PartitionSpec as P

SEQ_LEN = 256
MESH = pl.DeviceIdType.MESH


retain_weight = 2.0


DP = ("yh", "z", "core")
ALL_AXES = DP + ("shard",)


def device_on(axis, index):
    return tuple(index if a == axis else lax.axis_index(a) for a in ALL_AXES)


def gather_kernel(axis, n, part, x_ref, out_ref, send_sem, recv_sem):
    me = lax.axis_index(axis)

    barrier = pltpu.get_barrier_semaphore()
    for off in range(1, n):
        peer = lax.rem(me + off, n)
        pl.semaphore_signal(barrier, inc=1, device_id=device_on(axis, peer), device_id_type=MESH)
    pl.semaphore_wait(barrier, n - 1)

    copies = []
    for off in range(1, n):
        peer = lax.rem(me + off, n)
        copy = pltpu.make_async_remote_copy(
            src_ref=x_ref.at[part],
            dst_ref=out_ref.at[me],
            send_sem=send_sem.at[off - 1],
            recv_sem=recv_sem.at[me],
            device_id=device_on(axis, peer),
            device_id_type=MESH,
        )
        copy.start()
        copies.append(copy)
    for copy in copies:
        copy.wait_send()
    for off in range(1, n):
        src = lax.rem(me + n - off, n)
        arrival = pltpu.make_async_remote_copy(
            src_ref=x_ref.at[part],
            dst_ref=out_ref.at[src],
            send_sem=send_sem.at[off - 1],
            recv_sem=recv_sem.at[src],
            device_id=device_on(axis, src),
            device_id_type=MESH,
        )
        arrival.wait_recv()


def placed_gather_kernel(n, n_zhi, part, x_ref, out_ref, send_sem, recv_sem):
    me = lax.axis_index("shard")

    def where(j):
        return out_ref.at[:, pl.ds(2 * lax.rem(j, n_zhi), 2), pl.ds(j // n_zhi, 1)]

    barrier = pltpu.get_barrier_semaphore()
    for off in range(1, n):
        peer = lax.rem(me + off, n)
        pl.semaphore_signal(barrier, inc=1, device_id=device_on("shard", peer), device_id_type=MESH)
    pl.semaphore_wait(barrier, n - 1)

    copies = []
    for off in range(1, n):
        peer = lax.rem(me + off, n)
        copy = pltpu.make_async_remote_copy(
            src_ref=x_ref.at[part],
            dst_ref=where(me),
            send_sem=send_sem.at[off - 1],
            recv_sem=recv_sem.at[me],
            device_id=device_on("shard", peer),
            device_id_type=MESH,
        )
        copy.start()
        copies.append(copy)
    for copy in copies:
        copy.wait_send()
    for off in range(1, n):
        src = lax.rem(me + n - off, n)
        arrival = pltpu.make_async_remote_copy(
            src_ref=x_ref.at[part],
            dst_ref=where(src),
            send_sem=send_sem.at[off - 1],
            recv_sem=recv_sem.at[src],
            device_id=device_on("shard", src),
            device_id_type=MESH,
        )
        arrival.wait_recv()


def gather_part(xt, part, collective_id, out_dims):
    n = lax.axis_size("shard")
    n_zhi = out_dims[1] // 2
    received = pl.pallas_call(
        functools.partial(placed_gather_kernel, n, n_zhi, part),
        out_shape=jax.ShapeDtypeStruct(out_dims, xt.dtype),
        in_specs=[pl.BlockSpec(memory_space=pl.ANY)],
        out_specs=pl.BlockSpec(memory_space=pl.ANY),
        scratch_shapes=[pltpu.SemaphoreType.DMA((n - 1,)), pltpu.SemaphoreType.DMA((n,))],
        compiler_params=pltpu.CompilerParams(collective_id=collective_id, has_side_effects=True),
        cost_estimate=pl.CostEstimate(
            flops=0, bytes_accessed=2 * n * xt[part].nbytes, transcendentals=0
        ),
    )(xt)
    me = lax.axis_index("shard")
    at = (0, 2 * lax.rem(me, n_zhi), me // n_zhi, 0, 0)
    return lax.dynamic_update_slice(received, xt[part], at)


def swap_kernel(axis, halves, x_ref, out_ref, send_sem, recv_sem):
    me = lax.axis_index(axis)
    partner = device_on(axis, 1 - me)

    barrier = pltpu.get_barrier_semaphore()
    pl.semaphore_signal(barrier, inc=1, device_id=partner, device_id_type=MESH)
    pl.semaphore_wait(barrier, 1)

    copy = pltpu.make_async_remote_copy(
        src_ref=x_ref.at[1 - me] if halves else x_ref,
        dst_ref=out_ref,
        send_sem=send_sem,
        recv_sem=recv_sem,
        device_id=partner,
        device_id_type=MESH,
    )
    copy.start()
    copy.wait()


def swap_with_partner(x, collective_id, halves, axis="core"):
    return pl.pallas_call(
        functools.partial(swap_kernel, axis, halves),
        out_shape=jax.ShapeDtypeStruct(x.shape[1:] if halves else x.shape, x.dtype),
        in_specs=[pl.BlockSpec(memory_space=pl.ANY)],
        out_specs=pl.BlockSpec(memory_space=pl.ANY),
        scratch_shapes=[pltpu.SemaphoreType.DMA(()), pltpu.SemaphoreType.DMA(())],
        compiler_params=pltpu.CompilerParams(collective_id=collective_id, has_side_effects=True),
    )(x)


def ring_gather_kernel(axis, n, x_ref, out_ref, send_sem, recv_sem):
    me = lax.axis_index(axis)
    right, left = lax.rem(me + 1, n), lax.rem(me + n - 1, n)

    barrier = pltpu.get_barrier_semaphore()
    for neighbour in (left, right):
        pl.semaphore_signal(barrier, inc=1, device_id=device_on(axis, neighbour), device_id_type=MESH)
    pl.semaphore_wait(barrier, 2)

    def arrival(slot):
        return pltpu.make_async_remote_copy(
            src_ref=x_ref,
            dst_ref=out_ref.at[slot],
            send_sem=send_sem.at[0, 0],
            recv_sem=recv_sem.at[slot],
            device_id=device_on(axis, left),
            device_id_type=MESH,
        )

    copies = []
    steps = (n // 2, (n - 1) // 2)
    for k in range(max(steps)):
        for ring, (sign, target) in enumerate(((-1, right), (1, left))):
            if k >= steps[ring]:
                continue
            slot = lax.rem(me + sign * k + n, n)
            if k > 0:
                arrival(slot).wait_recv()
            copy = pltpu.make_async_remote_copy(
                src_ref=x_ref if k == 0 else out_ref.at[slot],
                dst_ref=out_ref.at[slot],
                send_sem=send_sem.at[ring, k],
                recv_sem=recv_sem.at[slot],
                device_id=device_on(axis, target),
                device_id_type=MESH,
            )
            copy.start()
            copies.append(copy)
    arrival(lax.rem(me - steps[0] + n, n)).wait_recv()
    arrival(lax.rem(me + steps[1], n)).wait_recv()
    for copy in copies:
        copy.wait_send()


def ring_gather(x, axis, collective_id):
    n = lax.axis_size(axis)
    received = pl.pallas_call(
        functools.partial(ring_gather_kernel, axis, n),
        out_shape=jax.ShapeDtypeStruct((n,) + x.shape, x.dtype),
        in_specs=[pl.BlockSpec(memory_space=pl.ANY)],
        out_specs=pl.BlockSpec(memory_space=pl.ANY),
        scratch_shapes=[pltpu.SemaphoreType.DMA((2, n // 2)), pltpu.SemaphoreType.DMA((n,))],
        compiler_params=pltpu.CompilerParams(collective_id=collective_id, has_side_effects=True),
    )(x)
    whole = lax.dynamic_update_index_in_dim(received, x, lax.axis_index(axis), 0)
    return whole.reshape((n * x.shape[0],) + x.shape[1:])


def per_device(resid_in, hidden, w_down, frozen, steer, forget_flags):
    n_yh, n_z, n_c = (lax.axis_size(a) for a in DP)
    tok_rows, d_cols = resid_in.shape
    own_tokens, ff_rows = hidden.shape
    n_parts = 4
    sub = tok_rows // n_parts
    blocks = own_tokens // tok_rows
    total_tokens = own_tokens * lax.axis_size("shard")
    me_c = lax.axis_index("core")
    me_yh = lax.axis_index("yh")
    xt = hidden.reshape(blocks // n_c, n_c, n_parts, 1, sub, ff_rows).transpose(2, 1, 0, 3, 4, 5)
    hp_parts, mlp_parts = [], []
    pair_w = jnp.concatenate([w_down, swap_with_partner(w_down, 4 * n_parts, False)], axis=0)
    for part in range(n_parts):
        if part > 0:
            xt, _ = lax.optimization_barrier((xt, reduced))
        got = gather_part(xt, part, 2 * part, (n_c, n_z, n_yh, sub, ff_rows))
        hp = got.reshape(n_c, n_z * n_yh * sub, ff_rows)
        hp_parts.append(hp)
        from_partner = swap_with_partner(hp, 2 * part + 1, True)
        pair_rows = jnp.concatenate([hp[me_c], from_partner], axis=1)
        reduced = jnp.dot(pair_rows, pair_w, preferred_element_type=jnp.float32)
        reduced_z = lax.psum_scatter(reduced, "z", scatter_dimension=0, tiled=True)
        by_yh = reduced_z.reshape((n_yh, -1, d_cols))
        mlp_parts.append(by_yh[me_yh] + swap_with_partner(by_yh, 2 * n_parts + part, True, "yh"))
    mlp_out = jnp.concatenate(mlp_parts, axis=0)
    residual = resid_in.astype(jnp.float32) + mlp_out
    updated = residual.astype(jnp.bfloat16)
    target_rows = lax.all_to_all(frozen, "shard", split_axis=1, concat_axis=0, tiled=True)
    row_block = (lax.axis_index("yh") * n_z + lax.axis_index("z")) * n_c + me_c
    start_row = row_block * tok_rows
    seq_ids = (start_row + jnp.arange(tok_rows, dtype=jnp.int32)) // SEQ_LEN
    seq_match = seq_ids[:, None] == jnp.arange(forget_flags.shape[0], dtype=jnp.int32)[None, :]
    is_forget = jnp.sum(jnp.where(seq_match, forget_flags[None, :], 0), axis=1) > 0
    target = jnp.where(
        is_forget[:, None], steer.astype(jnp.float32)[None, :], target_rows.astype(jnp.float32)
    )
    loss_weight = jnp.where(is_forget, 1.0, retain_weight).astype(jnp.float32)
    slopes = (loss_weight[:, None] * (residual - target) * (1.0 / math.sqrt(total_tokens))).astype(
        jnp.bfloat16
    )
    other_yh = swap_with_partner(slopes, 3 * n_parts, False, "yh")
    gathered = jnp.where(
        me_yh == 0,
        jnp.concatenate([slopes, other_yh], axis=0),
        jnp.concatenate([other_yh, slopes], axis=0),
    )
    gathered = ring_gather(gathered, "z", 3 * n_parts + 1)
    partner_slopes = swap_with_partner(gathered, 3 * n_parts + 2, False)
    contract = (((0,), (0,)), ((), ()))
    grad_down = None
    for part in range(n_parts):
        for rows, got in ((me_c, gathered), (1 - me_c, partner_slopes)):
            s_part = got.reshape(n_z * n_yh, n_parts, sub, d_cols)[:, part].reshape(-1, d_cols)
            term = lax.dot_general(
                lax.dynamic_index_in_dim(hp_parts[part], rows, keepdims=False),
                s_part,
                contract,
                preferred_element_type=jnp.float32,
            )
            grad_down = term if grad_down is None else grad_down + term
    return (updated, grad_down)


def solution(mesh):
    n_dp, n_shard = mesh.devices.shape
    n_z = 8
    parts = mesh.devices.reshape(n_dp // (2 * n_z), n_z, 2, n_shard)
    split_mesh = Mesh(parts, DP + ("shard",))
    in_specs = (
        P(DP, "shard"),
        P("shard", DP),
        P(DP, "shard"),
        P(DP + ("shard",), None),
        P("shard"),
        P(),
    )
    out_specs = (P(DP, "shard"), P(DP, "shard"))
    return jax.shard_map(
        per_device, mesh=split_mesh, in_specs=in_specs, out_specs=out_specs, check_vma=False
    )
```

```python
import functools
import math

import jax
import jax.numpy as jnp
from jax import lax
from jax.experimental import pallas as pl
from jax.experimental.pallas import tpu as pltpu
from jax.sharding import Mesh, PartitionSpec as P

SEQ_LEN = 256
MESH = pl.DeviceIdType.MESH


retain_weight = 2.0


DP = ("yh", "z", "core")
ALL_AXES = DP + ("shard",)


def device_on(axis, index):
    return tuple(index if a == axis else lax.axis_index(a) for a in ALL_AXES)


def gather_kernel(axis, n, part, x_ref, out_ref, send_sem, recv_sem):
    me = lax.axis_index(axis)

    barrier = pltpu.get_barrier_semaphore()
    for off in range(1, n):
        peer = lax.rem(me + off, n)
        pl.semaphore_signal(barrier, inc=1, device_id=device_on(axis, peer), device_id_type=MESH)
    pl.semaphore_wait(barrier, n - 1)

    copies = []
    for off in range(1, n):
        peer = lax.rem(me + off, n)
        copy = pltpu.make_async_remote_copy(
            src_ref=x_ref.at[part],
            dst_ref=out_ref.at[me],
            send_sem=send_sem.at[off - 1],
            recv_sem=recv_sem.at[me],
            device_id=device_on(axis, peer),
            device_id_type=MESH,
        )
        copy.start()
        copies.append(copy)
    for copy in copies:
        copy.wait_send()
    for off in range(1, n):
        src = lax.rem(me + n - off, n)
        arrival = pltpu.make_async_remote_copy(
            src_ref=x_ref.at[part],
            dst_ref=out_ref.at[src],
            send_sem=send_sem.at[off - 1],
            recv_sem=recv_sem.at[src],
            device_id=device_on(axis, src),
            device_id_type=MESH,
        )
        arrival.wait_recv()


def placed_gather_kernel(n, n_zhi, part, with_w, *refs):
    if with_w:
        x_ref, w_ref, out_ref, w_out, send_sem, recv_sem, w_sem = refs
    else:
        x_ref, out_ref, send_sem, recv_sem = refs
    me = lax.axis_index("shard")
    partner = device_on("core", 1 - lax.axis_index("core"))

    def where(j):
        return out_ref.at[:, pl.ds(2 * lax.rem(j, n_zhi), 2), pl.ds(j // n_zhi, 1)]

    barrier = pltpu.get_barrier_semaphore()
    for off in range(1, n):
        peer = lax.rem(me + off, n)
        pl.semaphore_signal(barrier, inc=1, device_id=device_on("shard", peer), device_id_type=MESH)
    if with_w:
        pl.semaphore_signal(barrier, inc=1, device_id=partner, device_id_type=MESH)
    pl.semaphore_wait(barrier, n if with_w else n - 1)

    if with_w:
        w_copy = pltpu.make_async_remote_copy(
            src_ref=w_ref,
            dst_ref=w_out,
            send_sem=w_sem.at[0],
            recv_sem=w_sem.at[1],
            device_id=partner,
            device_id_type=MESH,
        )
        w_copy.start()
    copies = []
    for off in range(1, n):
        peer = lax.rem(me + off, n)
        copy = pltpu.make_async_remote_copy(
            src_ref=x_ref.at[part],
            dst_ref=where(me),
            send_sem=send_sem.at[off - 1],
            recv_sem=recv_sem.at[me],
            device_id=device_on("shard", peer),
            device_id_type=MESH,
        )
        copy.start()
        copies.append(copy)
    for copy in copies:
        copy.wait_send()
    for off in range(1, n):
        src = lax.rem(me + n - off, n)
        arrival = pltpu.make_async_remote_copy(
            src_ref=x_ref.at[part],
            dst_ref=where(src),
            send_sem=send_sem.at[off - 1],
            recv_sem=recv_sem.at[src],
            device_id=device_on("shard", src),
            device_id_type=MESH,
        )
        arrival.wait_recv()
    if with_w:
        w_copy.wait()


def gather_part(xt, part, collective_id, out_dims, w=None):
    n = lax.axis_size("shard")
    n_zhi = out_dims[1] // 2
    with_w = w is not None
    operands = (xt, w) if with_w else (xt,)
    out_shape = [jax.ShapeDtypeStruct(out_dims, xt.dtype)]
    scratch = [pltpu.SemaphoreType.DMA((n - 1,)), pltpu.SemaphoreType.DMA((n,))]
    if with_w:
        out_shape.append(jax.ShapeDtypeStruct(w.shape, w.dtype))
        scratch.append(pltpu.SemaphoreType.DMA((2,)))
    results = pl.pallas_call(
        functools.partial(placed_gather_kernel, n, n_zhi, part, with_w),
        out_shape=tuple(out_shape),
        in_specs=[pl.BlockSpec(memory_space=pl.ANY)] * len(operands),
        out_specs=tuple(pl.BlockSpec(memory_space=pl.ANY) for _ in out_shape),
        scratch_shapes=scratch,
        compiler_params=pltpu.CompilerParams(collective_id=collective_id, has_side_effects=True),
        cost_estimate=pl.CostEstimate(
            flops=0, bytes_accessed=2 * n * xt[part].nbytes, transcendentals=0
        ),
    )(*operands)
    me = lax.axis_index("shard")
    at = (0, 2 * lax.rem(me, n_zhi), me // n_zhi, 0, 0)
    whole = lax.dynamic_update_slice(results[0], xt[part], at)
    return (whole, results[1]) if with_w else whole


def swap_kernel(axis, halves, x_ref, out_ref, send_sem, recv_sem):
    me = lax.axis_index(axis)
    partner = device_on(axis, 1 - me)

    barrier = pltpu.get_barrier_semaphore()
    pl.semaphore_signal(barrier, inc=1, device_id=partner, device_id_type=MESH)
    pl.semaphore_wait(barrier, 1)

    copy = pltpu.make_async_remote_copy(
        src_ref=x_ref.at[1 - me] if halves else x_ref,
        dst_ref=out_ref,
        send_sem=send_sem,
        recv_sem=recv_sem,
        device_id=partner,
        device_id_type=MESH,
    )
    copy.start()
    copy.wait()


def swap_with_partner(x, collective_id, halves, axis="core"):
    return pl.pallas_call(
        functools.partial(swap_kernel, axis, halves),
        out_shape=jax.ShapeDtypeStruct(x.shape[1:] if halves else x.shape, x.dtype),
        in_specs=[pl.BlockSpec(memory_space=pl.ANY)],
        out_specs=pl.BlockSpec(memory_space=pl.ANY),
        scratch_shapes=[pltpu.SemaphoreType.DMA(()), pltpu.SemaphoreType.DMA(())],
        compiler_params=pltpu.CompilerParams(collective_id=collective_id, has_side_effects=True),
    )(x)


def ring_gather_kernel(axis, n, x_ref, out_ref, send_sem, recv_sem):
    me = lax.axis_index(axis)
    right, left = lax.rem(me + 1, n), lax.rem(me + n - 1, n)

    barrier = pltpu.get_barrier_semaphore()
    for neighbour in (left, right):
        pl.semaphore_signal(barrier, inc=1, device_id=device_on(axis, neighbour), device_id_type=MESH)
    pl.semaphore_wait(barrier, 2)

    def arrival(slot):
        return pltpu.make_async_remote_copy(
            src_ref=x_ref,
            dst_ref=out_ref.at[slot],
            send_sem=send_sem.at[0, 0],
            recv_sem=recv_sem.at[slot],
            device_id=device_on(axis, left),
            device_id_type=MESH,
        )

    copies = []
    steps = (n // 2, (n - 1) // 2)
    for k in range(max(steps)):
        for ring, (sign, target) in enumerate(((-1, right), (1, left))):
            if k >= steps[ring]:
                continue
            slot = lax.rem(me + sign * k + n, n)
            if k > 0:
                arrival(slot).wait_recv()
            copy = pltpu.make_async_remote_copy(
                src_ref=x_ref if k == 0 else out_ref.at[slot],
                dst_ref=out_ref.at[slot],
                send_sem=send_sem.at[ring, k],
                recv_sem=recv_sem.at[slot],
                device_id=device_on(axis, target),
                device_id_type=MESH,
            )
            copy.start()
            copies.append(copy)
    arrival(lax.rem(me - steps[0] + n, n)).wait_recv()
    arrival(lax.rem(me + steps[1], n)).wait_recv()
    for copy in copies:
        copy.wait_send()


def ring_gather(x, axis, collective_id):
    n = lax.axis_size(axis)
    received = pl.pallas_call(
        functools.partial(ring_gather_kernel, axis, n),
        out_shape=jax.ShapeDtypeStruct((n,) + x.shape, x.dtype),
        in_specs=[pl.BlockSpec(memory_space=pl.ANY)],
        out_specs=pl.BlockSpec(memory_space=pl.ANY),
        scratch_shapes=[pltpu.SemaphoreType.DMA((2, n // 2)), pltpu.SemaphoreType.DMA((n,))],
        compiler_params=pltpu.CompilerParams(collective_id=collective_id, has_side_effects=True),
    )(x)
    whole = lax.dynamic_update_index_in_dim(received, x, lax.axis_index(axis), 0)
    return whole.reshape((n * x.shape[0],) + x.shape[1:])


def per_device(resid_in, hidden, w_down, frozen, steer, forget_flags):
    n_yh, n_z, n_c = (lax.axis_size(a) for a in DP)
    tok_rows, d_cols = resid_in.shape
    own_tokens, ff_rows = hidden.shape
    n_parts = 2
    sub = tok_rows // n_parts
    blocks = own_tokens // tok_rows
    total_tokens = own_tokens * lax.axis_size("shard")
    me_c = lax.axis_index("core")
    me_yh = lax.axis_index("yh")
    xt = hidden.reshape(blocks // n_c, n_c, n_parts, 1, sub, ff_rows).transpose(2, 1, 0, 3, 4, 5)
    hp_parts, mlp_parts = [], []
    for part in range(n_parts):
        if part > 0:
            xt, _ = lax.optimization_barrier((xt, reduced))
        if part == 0:
            got, partner_w = gather_part(xt, part, 0, (n_c, n_z, n_yh, sub, ff_rows), w_down)
            pair_w = jnp.concatenate([w_down, partner_w], axis=0)
        else:
            got = gather_part(xt, part, 2 * part, (n_c, n_z, n_yh, sub, ff_rows))
        hp = got.reshape(n_c, n_z * n_yh * sub, ff_rows)
        hp_parts.append(hp)
        from_partner = swap_with_partner(hp, 2 * part + 1, True)
        pair_rows = jnp.concatenate([hp[me_c], from_partner], axis=1)
        reduced = jnp.dot(pair_rows, pair_w, preferred_element_type=jnp.float32)
        reduced_z = lax.psum_scatter(reduced, "z", scatter_dimension=0, tiled=True)
        by_yh = reduced_z.reshape((n_yh, -1, d_cols))
        mlp_parts.append(by_yh[me_yh] + swap_with_partner(by_yh, 6 + part, True, "yh"))
    mlp_out = jnp.concatenate(mlp_parts, axis=0)
    residual = resid_in.astype(jnp.float32) + mlp_out
    updated = residual.astype(jnp.bfloat16)
    target_rows = lax.all_to_all(frozen, "shard", split_axis=1, concat_axis=0, tiled=True)
    row_block = (lax.axis_index("yh") * n_z + lax.axis_index("z")) * n_c + me_c
    start_row = row_block * tok_rows
    seq_ids = (start_row + jnp.arange(tok_rows, dtype=jnp.int32)) // SEQ_LEN
    seq_match = seq_ids[:, None] == jnp.arange(forget_flags.shape[0], dtype=jnp.int32)[None, :]
    is_forget = jnp.sum(jnp.where(seq_match, forget_flags[None, :], 0), axis=1) > 0
    target = jnp.where(
        is_forget[:, None], steer.astype(jnp.float32)[None, :], target_rows.astype(jnp.float32)
    )
    loss_weight = jnp.where(is_forget, 1.0, retain_weight).astype(jnp.float32)
    slopes = (loss_weight[:, None] * (residual - target) * (1.0 / math.sqrt(total_tokens))).astype(
        jnp.bfloat16
    )
    other_yh = swap_with_partner(slopes, 6 + n_parts, False, "yh")
    gathered = jnp.where(
        me_yh == 0,
        jnp.concatenate([slopes, other_yh], axis=0),
        jnp.concatenate([other_yh, slopes], axis=0),
    )
    gathered = ring_gather(gathered, "z", 10)
    partner_slopes = swap_with_partner(gathered, 2 * n_parts + 1, False)
    contract = (((0,), (0,)), ((), ()))
    grad_down = None
    for part in range(n_parts):
        for rows, got in ((me_c, gathered), (1 - me_c, partner_slopes)):
            s_part = got.reshape(n_z * n_yh, n_parts, sub, d_cols)[:, part].reshape(-1, d_cols)
            term = lax.dot_general(
                lax.dynamic_index_in_dim(hp_parts[part], rows, keepdims=False),
                s_part,
                contract,
                preferred_element_type=jnp.float32,
            )
            grad_down = term if grad_down is None else grad_down + term
    return (updated, grad_down)


def solution(mesh):
    n_dp, n_shard = mesh.devices.shape
    n_z = 8
    parts = mesh.devices.reshape(n_dp // (2 * n_z), n_z, 2, n_shard)
    split_mesh = Mesh(parts, DP + ("shard",))
    in_specs = (
        P(DP, "shard"),
        P("shard", DP),
        P(DP, "shard"),
        P(DP + ("shard",), None),
        P("shard"),
        P(),
    )
    out_specs = (P(DP, "shard"), P(DP, "shard"))
    return jax.shard_map(
        per_device, mesh=split_mesh, in_specs=in_specs, out_specs=out_specs, check_vma=False
    )
```

```python
import functools
import math

import jax
import jax.numpy as jnp
from jax import lax
from jax.experimental import pallas as pl
from jax.experimental.pallas import tpu as pltpu
from jax.sharding import Mesh, PartitionSpec as P

SEQ_LEN = 256
MESH = pl.DeviceIdType.MESH


retain_weight = 2.0


DP = ("yh", "z", "core")
ALL_AXES = DP + ("shard",)


def device_on(axis, index):
    return tuple(index if a == axis else lax.axis_index(a) for a in ALL_AXES)


def gather_kernel(axis, n, part, x_ref, out_ref, send_sem, recv_sem):
    me = lax.axis_index(axis)

    barrier = pltpu.get_barrier_semaphore()
    for off in range(1, n):
        peer = lax.rem(me + off, n)
        pl.semaphore_signal(barrier, inc=1, device_id=device_on(axis, peer), device_id_type=MESH)
    pl.semaphore_wait(barrier, n - 1)

    copies = []
    for off in range(1, n):
        peer = lax.rem(me + off, n)
        copy = pltpu.make_async_remote_copy(
            src_ref=x_ref.at[part],
            dst_ref=out_ref.at[me],
            send_sem=send_sem.at[off - 1],
            recv_sem=recv_sem.at[me],
            device_id=device_on(axis, peer),
            device_id_type=MESH,
        )
        copy.start()
        copies.append(copy)
    for copy in copies:
        copy.wait_send()
    for off in range(1, n):
        src = lax.rem(me + n - off, n)
        arrival = pltpu.make_async_remote_copy(
            src_ref=x_ref.at[part],
            dst_ref=out_ref.at[src],
            send_sem=send_sem.at[off - 1],
            recv_sem=recv_sem.at[src],
            device_id=device_on(axis, src),
            device_id_type=MESH,
        )
        arrival.wait_recv()


def placed_gather_kernel(n, n_zhi, part, x_ref, out_ref, send_sem, recv_sem):
    me = lax.axis_index("shard")

    def where(j):
        return out_ref.at[:, pl.ds(2 * lax.rem(j, n_zhi), 2), pl.ds(j // n_zhi, 1)]

    barrier = pltpu.get_barrier_semaphore()
    for off in range(1, n):
        peer = lax.rem(me + off, n)
        pl.semaphore_signal(barrier, inc=1, device_id=device_on("shard", peer), device_id_type=MESH)
    pl.semaphore_wait(barrier, n - 1)

    copies = []
    for off in range(1, n):
        peer = lax.rem(me + off, n)
        copy = pltpu.make_async_remote_copy(
            src_ref=x_ref.at[part],
            dst_ref=where(me),
            send_sem=send_sem.at[off - 1],
            recv_sem=recv_sem.at[me],
            device_id=device_on("shard", peer),
            device_id_type=MESH,
        )
        copy.start()
        copies.append(copy)
    for copy in copies:
        copy.wait_send()
    for off in range(1, n):
        src = lax.rem(me + n - off, n)
        arrival = pltpu.make_async_remote_copy(
            src_ref=x_ref.at[part],
            dst_ref=where(src),
            send_sem=send_sem.at[off - 1],
            recv_sem=recv_sem.at[src],
            device_id=device_on("shard", src),
            device_id_type=MESH,
        )
        arrival.wait_recv()


def gather_part(xt, part, collective_id, out_dims):
    n = lax.axis_size("shard")
    n_zhi = out_dims[1] // 2
    received = pl.pallas_call(
        functools.partial(placed_gather_kernel, n, n_zhi, part),
        out_shape=jax.ShapeDtypeStruct(out_dims, xt.dtype),
        in_specs=[pl.BlockSpec(memory_space=pl.ANY)],
        out_specs=pl.BlockSpec(memory_space=pl.ANY),
        scratch_shapes=[pltpu.SemaphoreType.DMA((n - 1,)), pltpu.SemaphoreType.DMA((n,))],
        compiler_params=pltpu.CompilerParams(collective_id=collective_id, has_side_effects=True),
        cost_estimate=pl.CostEstimate(
            flops=0, bytes_accessed=2 * n * xt[part].nbytes, transcendentals=0
        ),
    )(xt)
    me = lax.axis_index("shard")
    at = (0, 2 * lax.rem(me, n_zhi), me // n_zhi, 0, 0)
    return lax.dynamic_update_slice(received, xt[part], at)


def swap_kernel(axis, halves, x_ref, out_ref, send_sem, recv_sem):
    me = lax.axis_index(axis)
    partner = device_on(axis, 1 - me)

    barrier = pltpu.get_barrier_semaphore()
    pl.semaphore_signal(barrier, inc=1, device_id=partner, device_id_type=MESH)
    pl.semaphore_wait(barrier, 1)

    copy = pltpu.make_async_remote_copy(
        src_ref=x_ref.at[1 - me] if halves else x_ref,
        dst_ref=out_ref,
        send_sem=send_sem,
        recv_sem=recv_sem,
        device_id=partner,
        device_id_type=MESH,
    )
    copy.start()
    copy.wait()


def swap_with_partner(x, collective_id, halves, axis="core"):
    return pl.pallas_call(
        functools.partial(swap_kernel, axis, halves),
        out_shape=jax.ShapeDtypeStruct(x.shape[1:] if halves else x.shape, x.dtype),
        in_specs=[pl.BlockSpec(memory_space=pl.ANY)],
        out_specs=pl.BlockSpec(memory_space=pl.ANY),
        scratch_shapes=[pltpu.SemaphoreType.DMA(()), pltpu.SemaphoreType.DMA(())],
        compiler_params=pltpu.CompilerParams(collective_id=collective_id, has_side_effects=True),
    )(x)


def ring_gather_kernel(axis, n, x_ref, out_ref, pair_ref, send_sem, recv_sem, pair_send, pair_recv):
    me = lax.axis_index(axis)
    right, left = lax.rem(me + 1, n), lax.rem(me + n - 1, n)
    partner = device_on("core", 1 - lax.axis_index("core"))

    barrier = pltpu.get_barrier_semaphore()
    for neighbour in (left, right):
        pl.semaphore_signal(barrier, inc=1, device_id=device_on(axis, neighbour), device_id_type=MESH)
    pl.semaphore_signal(barrier, inc=1, device_id=partner, device_id_type=MESH)
    pl.semaphore_wait(barrier, 3)

    def arrival(slot):
        return pltpu.make_async_remote_copy(
            src_ref=x_ref,
            dst_ref=out_ref.at[slot],
            send_sem=send_sem.at[0, 0],
            recv_sem=recv_sem.at[slot],
            device_id=device_on(axis, left),
            device_id_type=MESH,
        )

    def to_partner(src, slot):
        return pltpu.make_async_remote_copy(
            src_ref=src,
            dst_ref=pair_ref.at[slot],
            send_sem=pair_send.at[slot],
            recv_sem=pair_recv.at[slot],
            device_id=partner,
            device_id_type=MESH,
        )

    copies = []
    own = to_partner(x_ref, me)
    own.start()
    copies.append(own)
    steps = (n // 2, (n - 1) // 2)
    for k in range(max(steps)):
        for ring, (sign, target) in enumerate(((-1, right), (1, left))):
            if k >= steps[ring]:
                continue
            slot = lax.rem(me + sign * k + n, n)
            if k > 0:
                arrival(slot).wait_recv()
                forward = to_partner(out_ref.at[slot], slot)
                forward.start()
                copies.append(forward)
            copy = pltpu.make_async_remote_copy(
                src_ref=x_ref if k == 0 else out_ref.at[slot],
                dst_ref=out_ref.at[slot],
                send_sem=send_sem.at[ring, k],
                recv_sem=recv_sem.at[slot],
                device_id=device_on(axis, target),
                device_id_type=MESH,
            )
            copy.start()
            copies.append(copy)
    for slot in (lax.rem(me - steps[0] + n, n), lax.rem(me + steps[1], n)):
        arrival(slot).wait_recv()
        forward = to_partner(out_ref.at[slot], slot)
        forward.start()
        copies.append(forward)
    for copy in copies:
        copy.wait_send()
    for slot in range(n):
        to_partner(x_ref, slot).wait_recv()


def ring_gather(x, axis, collective_id):
    n = lax.axis_size(axis)
    received, from_partner = pl.pallas_call(
        functools.partial(ring_gather_kernel, axis, n),
        out_shape=(
            jax.ShapeDtypeStruct((n,) + x.shape, x.dtype),
            jax.ShapeDtypeStruct((n,) + x.shape, x.dtype),
        ),
        in_specs=[pl.BlockSpec(memory_space=pl.ANY)],
        out_specs=(pl.BlockSpec(memory_space=pl.ANY), pl.BlockSpec(memory_space=pl.ANY)),
        scratch_shapes=[
            pltpu.SemaphoreType.DMA((2, n // 2)),
            pltpu.SemaphoreType.DMA((n,)),
            pltpu.SemaphoreType.DMA((n,)),
            pltpu.SemaphoreType.DMA((n,)),
        ],
        compiler_params=pltpu.CompilerParams(collective_id=collective_id, has_side_effects=True),
    )(x)
    whole = lax.dynamic_update_index_in_dim(received, x, lax.axis_index(axis), 0)
    rows = (n * x.shape[0],) + x.shape[1:]
    return whole.reshape(rows), from_partner.reshape(rows)


def per_device(resid_in, hidden, w_down, frozen, steer, forget_flags):
    n_yh, n_z, n_c = (lax.axis_size(a) for a in DP)
    tok_rows, d_cols = resid_in.shape
    own_tokens, ff_rows = hidden.shape
    n_parts = 2
    sub = tok_rows // n_parts
    blocks = own_tokens // tok_rows
    total_tokens = own_tokens * lax.axis_size("shard")
    me_c = lax.axis_index("core")
    me_yh = lax.axis_index("yh")
    xt = hidden.reshape(blocks // n_c, n_c, n_parts, 1, sub, ff_rows).transpose(2, 1, 0, 3, 4, 5)
    hp_parts, mlp_parts = [], []
    pair_w = jnp.concatenate([w_down, swap_with_partner(w_down, 9, False)], axis=0)
    for part in range(n_parts):
        if part > 0:
            xt, _ = lax.optimization_barrier((xt, reduced))
        got = gather_part(xt, part, 2 * part, (n_c, n_z, n_yh, sub, ff_rows))
        hp = got.reshape(n_c, n_z * n_yh * sub, ff_rows)
        hp_parts.append(hp)
        from_partner = swap_with_partner(hp, 2 * part + 1, True)
        pair_rows = jnp.concatenate([hp[me_c], from_partner], axis=1)
        reduced = jnp.dot(pair_rows, pair_w, preferred_element_type=jnp.float32)
        reduced_z = lax.psum_scatter(reduced, "z", scatter_dimension=0, tiled=True)
        by_yh = reduced_z.reshape((n_yh, -1, d_cols))
        mlp_parts.append(by_yh[me_yh] + swap_with_partner(by_yh, 6 + part, True, "yh"))
    mlp_out = jnp.concatenate(mlp_parts, axis=0)
    residual = resid_in.astype(jnp.float32) + mlp_out
    updated = residual.astype(jnp.bfloat16)
    target_rows = lax.all_to_all(frozen, "shard", split_axis=1, concat_axis=0, tiled=True)
    row_block = (lax.axis_index("yh") * n_z + lax.axis_index("z")) * n_c + me_c
    start_row = row_block * tok_rows
    seq_ids = (start_row + jnp.arange(tok_rows, dtype=jnp.int32)) // SEQ_LEN
    seq_match = seq_ids[:, None] == jnp.arange(forget_flags.shape[0], dtype=jnp.int32)[None, :]
    is_forget = jnp.sum(jnp.where(seq_match, forget_flags[None, :], 0), axis=1) > 0
    target = jnp.where(
        is_forget[:, None], steer.astype(jnp.float32)[None, :], target_rows.astype(jnp.float32)
    )
    loss_weight = jnp.where(is_forget, 1.0, retain_weight).astype(jnp.float32)
    slopes = (loss_weight[:, None] * (residual - target) * (1.0 / math.sqrt(total_tokens))).astype(
        jnp.bfloat16
    )
    other_yh = swap_with_partner(slopes, 6 + n_parts, False, "yh")
    gathered = jnp.where(
        me_yh == 0,
        jnp.concatenate([slopes, other_yh], axis=0),
        jnp.concatenate([other_yh, slopes], axis=0),
    )
    gathered, partner_slopes = ring_gather(gathered, "z", 10)
    contract = (((0,), (0,)), ((), ()))
    grad_down = None
    for part in range(n_parts):
        for rows, got in ((me_c, gathered), (1 - me_c, partner_slopes)):
            s_part = got.reshape(n_z * n_yh, n_parts, sub, d_cols)[:, part].reshape(-1, d_cols)
            term = lax.dot_general(
                lax.dynamic_index_in_dim(hp_parts[part], rows, keepdims=False),
                s_part,
                contract,
                preferred_element_type=jnp.float32,
            )
            grad_down = term if grad_down is None else grad_down + term
    return (updated, grad_down)


def solution(mesh):
    n_dp, n_shard = mesh.devices.shape
    n_z = 8
    parts = mesh.devices.reshape(n_dp // (2 * n_z), n_z, 2, n_shard)
    split_mesh = Mesh(parts, DP + ("shard",))
    in_specs = (
        P(DP, "shard"),
        P("shard", DP),
        P(DP, "shard"),
        P(DP + ("shard",), None),
        P("shard"),
        P(),
    )
    out_specs = (P(DP, "shard"), P(DP, "shard"))
    return jax.shard_map(
        per_device, mesh=split_mesh, in_specs=in_specs, out_specs=out_specs, check_vma=False
    )
```

```python
import functools
import math

import jax
import jax.numpy as jnp
from jax import lax
from jax.experimental import pallas as pl
from jax.experimental.pallas import tpu as pltpu
from jax.sharding import Mesh, PartitionSpec as P

SEQ_LEN = 256
MESH = pl.DeviceIdType.MESH


retain_weight = 2.0


DP = ("yh", "z", "core")
ALL_AXES = DP + ("shard",)


def device_on(axis, index):
    return tuple(index if a == axis else lax.axis_index(a) for a in ALL_AXES)


def gather_kernel(axis, n, part, x_ref, out_ref, send_sem, recv_sem):
    me = lax.axis_index(axis)

    barrier = pltpu.get_barrier_semaphore()
    for off in range(1, n):
        peer = lax.rem(me + off, n)
        pl.semaphore_signal(barrier, inc=1, device_id=device_on(axis, peer), device_id_type=MESH)
    pl.semaphore_wait(barrier, n - 1)

    copies = []
    for off in range(1, n):
        peer = lax.rem(me + off, n)
        copy = pltpu.make_async_remote_copy(
            src_ref=x_ref.at[part],
            dst_ref=out_ref.at[me],
            send_sem=send_sem.at[off - 1],
            recv_sem=recv_sem.at[me],
            device_id=device_on(axis, peer),
            device_id_type=MESH,
        )
        copy.start()
        copies.append(copy)
    for copy in copies:
        copy.wait_send()
    for off in range(1, n):
        src = lax.rem(me + n - off, n)
        arrival = pltpu.make_async_remote_copy(
            src_ref=x_ref.at[part],
            dst_ref=out_ref.at[src],
            send_sem=send_sem.at[off - 1],
            recv_sem=recv_sem.at[src],
            device_id=device_on(axis, src),
            device_id_type=MESH,
        )
        arrival.wait_recv()


def gather_along(x, axis, collective_id):
    n = lax.axis_size(axis)
    received = pl.pallas_call(
        functools.partial(gather_kernel, axis, n, 0),
        out_shape=jax.ShapeDtypeStruct((n,) + x.shape, x.dtype),
        in_specs=[pl.BlockSpec(memory_space=pl.ANY)],
        out_specs=pl.BlockSpec(memory_space=pl.ANY),
        scratch_shapes=[pltpu.SemaphoreType.DMA((n - 1,)), pltpu.SemaphoreType.DMA((n,))],
        compiler_params=pltpu.CompilerParams(collective_id=collective_id, has_side_effects=True),
    )(x[None])
    whole = lax.dynamic_update_index_in_dim(received, x, lax.axis_index(axis), 0)
    return whole.reshape((n * x.shape[0],) + x.shape[1:])


def placed_gather_kernel(n, n_zhi, part, x_ref, out_ref, send_sem, recv_sem):
    me = lax.axis_index("shard")

    def where(j):
        return out_ref.at[:, pl.ds(2 * lax.rem(j, n_zhi), 2), pl.ds(j // n_zhi, 1)]

    barrier = pltpu.get_barrier_semaphore()
    for off in range(1, n):
        peer = lax.rem(me + off, n)
        pl.semaphore_signal(barrier, inc=1, device_id=device_on("shard", peer), device_id_type=MESH)
    pl.semaphore_wait(barrier, n - 1)

    copies = []
    for off in range(1, n):
        peer = lax.rem(me + off, n)
        copy = pltpu.make_async_remote_copy(
            src_ref=x_ref.at[part],
            dst_ref=where(me),
            send_sem=send_sem.at[off - 1],
            recv_sem=recv_sem.at[me],
            device_id=device_on("shard", peer),
            device_id_type=MESH,
        )
        copy.start()
        copies.append(copy)
    for copy in copies:
        copy.wait_send()
    for off in range(1, n):
        src = lax.rem(me + n - off, n)
        arrival = pltpu.make_async_remote_copy(
            src_ref=x_ref.at[part],
            dst_ref=where(src),
            send_sem=send_sem.at[off - 1],
            recv_sem=recv_sem.at[src],
            device_id=device_on("shard", src),
            device_id_type=MESH,
        )
        arrival.wait_recv()


def gather_part(xt, part, collective_id, out_dims):
    n = lax.axis_size("shard")
    n_zhi = out_dims[1] // 2
    received = pl.pallas_call(
        functools.partial(placed_gather_kernel, n, n_zhi, part),
        out_shape=jax.ShapeDtypeStruct(out_dims, xt.dtype),
        in_specs=[pl.BlockSpec(memory_space=pl.ANY)],
        out_specs=pl.BlockSpec(memory_space=pl.ANY),
        scratch_shapes=[pltpu.SemaphoreType.DMA((n - 1,)), pltpu.SemaphoreType.DMA((n,))],
        compiler_params=pltpu.CompilerParams(collective_id=collective_id, has_side_effects=True),
        cost_estimate=pl.CostEstimate(
            flops=0, bytes_accessed=2 * n * xt[part].nbytes, transcendentals=0
        ),
    )(xt)
    me = lax.axis_index("shard")
    at = (0, 2 * lax.rem(me, n_zhi), me // n_zhi, 0, 0)
    return lax.dynamic_update_slice(received, xt[part], at)


def swap_kernel(axis, halves, x_ref, out_ref, send_sem, recv_sem):
    me = lax.axis_index(axis)
    partner = device_on(axis, 1 - me)

    barrier = pltpu.get_barrier_semaphore()
    pl.semaphore_signal(barrier, inc=1, device_id=partner, device_id_type=MESH)
    pl.semaphore_wait(barrier, 1)

    copy = pltpu.make_async_remote_copy(
        src_ref=x_ref.at[1 - me] if halves else x_ref,
        dst_ref=out_ref,
        send_sem=send_sem,
        recv_sem=recv_sem,
        device_id=partner,
        device_id_type=MESH,
    )
    copy.start()
    copy.wait()


def swap_with_partner(x, collective_id, halves, axis="core"):
    return pl.pallas_call(
        functools.partial(swap_kernel, axis, halves),
        out_shape=jax.ShapeDtypeStruct(x.shape[1:] if halves else x.shape, x.dtype),
        in_specs=[pl.BlockSpec(memory_space=pl.ANY)],
        out_specs=pl.BlockSpec(memory_space=pl.ANY),
        scratch_shapes=[pltpu.SemaphoreType.DMA(()), pltpu.SemaphoreType.DMA(())],
        compiler_params=pltpu.CompilerParams(collective_id=collective_id, has_side_effects=True),
    )(x)


def ring_gather_kernel(axis, n, x_ref, out_ref, pair_ref, send_sem, recv_sem, pair_send, pair_recv):
    me = lax.axis_index(axis)
    right, left = lax.rem(me + 1, n), lax.rem(me + n - 1, n)
    partner = device_on("core", 1 - lax.axis_index("core"))

    barrier = pltpu.get_barrier_semaphore()
    for neighbour in (left, right):
        pl.semaphore_signal(barrier, inc=1, device_id=device_on(axis, neighbour), device_id_type=MESH)
    pl.semaphore_signal(barrier, inc=1, device_id=partner, device_id_type=MESH)
    pl.semaphore_wait(barrier, 3)

    def arrival(slot):
        return pltpu.make_async_remote_copy(
            src_ref=x_ref,
            dst_ref=out_ref.at[slot],
            send_sem=send_sem.at[0, 0],
            recv_sem=recv_sem.at[slot],
            device_id=device_on(axis, left),
            device_id_type=MESH,
        )

    def to_partner(src, slot):
        return pltpu.make_async_remote_copy(
            src_ref=src,
            dst_ref=pair_ref.at[slot],
            send_sem=pair_send.at[slot],
            recv_sem=pair_recv.at[slot],
            device_id=partner,
            device_id_type=MESH,
        )

    copies = []
    own = to_partner(x_ref, me)
    own.start()
    copies.append(own)
    steps = (n // 2, (n - 1) // 2)
    for k in range(max(steps)):
        for ring, (sign, target) in enumerate(((-1, right), (1, left))):
            if k >= steps[ring]:
                continue
            slot = lax.rem(me + sign * k + n, n)
            if k > 0:
                arrival(slot).wait_recv()
                forward = to_partner(out_ref.at[slot], slot)
                forward.start()
                copies.append(forward)
            copy = pltpu.make_async_remote_copy(
                src_ref=x_ref if k == 0 else out_ref.at[slot],
                dst_ref=out_ref.at[slot],
                send_sem=send_sem.at[ring, k],
                recv_sem=recv_sem.at[slot],
                device_id=device_on(axis, target),
                device_id_type=MESH,
            )
            copy.start()
            copies.append(copy)
    for slot in (lax.rem(me - steps[0] + n, n), lax.rem(me + steps[1], n)):
        arrival(slot).wait_recv()
        forward = to_partner(out_ref.at[slot], slot)
        forward.start()
        copies.append(forward)
    for copy in copies:
        copy.wait_send()
    for slot in range(n):
        to_partner(x_ref, slot).wait_recv()


def ring_gather(x, axis, collective_id):
    n = lax.axis_size(axis)
    received, from_partner = pl.pallas_call(
        functools.partial(ring_gather_kernel, axis, n),
        out_shape=(
            jax.ShapeDtypeStruct((n,) + x.shape, x.dtype),
            jax.ShapeDtypeStruct((n,) + x.shape, x.dtype),
        ),
        in_specs=[pl.BlockSpec(memory_space=pl.ANY)],
        out_specs=(pl.BlockSpec(memory_space=pl.ANY), pl.BlockSpec(memory_space=pl.ANY)),
        scratch_shapes=[
            pltpu.SemaphoreType.DMA((2, n // 2)),
            pltpu.SemaphoreType.DMA((n,)),
            pltpu.SemaphoreType.DMA((n,)),
            pltpu.SemaphoreType.DMA((n,)),
        ],
        compiler_params=pltpu.CompilerParams(collective_id=collective_id, has_side_effects=True),
    )(x)
    whole = lax.dynamic_update_index_in_dim(received, x, lax.axis_index(axis), 0)
    rows = (n * x.shape[0],) + x.shape[1:]
    return whole.reshape(rows), from_partner.reshape(rows)


def per_device(resid_in, hidden, w_down, frozen, steer, forget_flags):
    n_yh, n_z, n_c = (lax.axis_size(a) for a in DP)
    tok_rows, d_cols = resid_in.shape
    own_tokens, ff_rows = hidden.shape
    n_parts = 2
    sub = tok_rows // n_parts
    blocks = own_tokens // tok_rows
    total_tokens = own_tokens * lax.axis_size("shard")
    me_c = lax.axis_index("core")
    me_yh = lax.axis_index("yh")
    xt = hidden.reshape(blocks // n_c, n_c, n_parts, 1, sub, ff_rows).transpose(2, 1, 0, 3, 4, 5)
    hp_parts, mlp_parts = [], []
    pair_w = jnp.concatenate([w_down, swap_with_partner(w_down, 9, False)], axis=0)
    for part in range(n_parts):
        if part > 0:
            xt, _ = lax.optimization_barrier((xt, reduced))
        got = gather_part(xt, part, 2 * part, (n_c, n_z, n_yh, sub, ff_rows))
        hp = got.reshape(n_c, n_z * n_yh * sub, ff_rows)
        hp_parts.append(hp)
        from_partner = swap_with_partner(hp, 2 * part + 1, True)
        pair_rows = jnp.concatenate([hp[me_c], from_partner], axis=1)
        reduced = jnp.dot(pair_rows, pair_w, preferred_element_type=jnp.float32)
        reduced_z = lax.psum_scatter(reduced, "z", scatter_dimension=0, tiled=True)
        by_yh = reduced_z.reshape((n_yh, -1, d_cols))
        mlp_parts.append(by_yh[me_yh] + swap_with_partner(by_yh, 6 + part, True, "yh"))
    mlp_out = jnp.concatenate(mlp_parts, axis=0)
    residual = resid_in.astype(jnp.float32) + mlp_out
    updated = residual.astype(jnp.bfloat16)
    target_rows = lax.all_to_all(frozen, "shard", split_axis=1, concat_axis=0, tiled=True)
    row_block = (lax.axis_index("yh") * n_z + lax.axis_index("z")) * n_c + me_c
    start_row = row_block * tok_rows
    seq_ids = (start_row + jnp.arange(tok_rows, dtype=jnp.int32)) // SEQ_LEN
    seq_match = seq_ids[:, None] == jnp.arange(forget_flags.shape[0], dtype=jnp.int32)[None, :]
    is_forget = jnp.sum(jnp.where(seq_match, forget_flags[None, :], 0), axis=1) > 0
    target = jnp.where(
        is_forget[:, None], steer.astype(jnp.float32)[None, :], target_rows.astype(jnp.float32)
    )
    loss_weight = jnp.where(is_forget, 1.0, retain_weight).astype(jnp.float32)
    slopes = (loss_weight[:, None] * (residual - target) * (1.0 / math.sqrt(total_tokens))).astype(
        jnp.bfloat16
    )
    gathered = gather_along(slopes, "yh", 6 + n_parts)
    gathered, partner_slopes = ring_gather(gathered, "z", 10)
    contract = (((0,), (0,)), ((), ()))
    grad_down = None
    for part in range(n_parts):
        for rows, got in ((me_c, gathered), (1 - me_c, partner_slopes)):
            s_part = got.reshape(n_z * n_yh, n_parts, sub, d_cols)[:, part].reshape(-1, d_cols)
            term = lax.dot_general(
                lax.dynamic_index_in_dim(hp_parts[part], rows, keepdims=False),
                s_part,
                contract,
                preferred_element_type=jnp.float32,
            )
            grad_down = term if grad_down is None else grad_down + term
    return (updated, grad_down)


def solution(mesh):
    n_dp, n_shard = mesh.devices.shape
    n_z = 8
    parts = mesh.devices.reshape(n_dp // (2 * n_z), n_z, 2, n_shard)
    split_mesh = Mesh(parts, DP + ("shard",))
    in_specs = (
        P(DP, "shard"),
        P("shard", DP),
        P(DP, "shard"),
        P(DP + ("shard",), None),
        P("shard"),
        P(),
    )
    out_specs = (P(DP, "shard"), P(DP, "shard"))
    return jax.shard_map(
        per_device, mesh=split_mesh, in_specs=in_specs, out_specs=out_specs, check_vma=False
    )
```

```python
import functools
import math

import jax
import jax.numpy as jnp
from jax import lax
from jax.experimental import pallas as pl
from jax.experimental.pallas import tpu as pltpu
from jax.sharding import Mesh, PartitionSpec as P

SEQ_LEN = 256
MESH = pl.DeviceIdType.MESH


retain_weight = 2.0


DP = ("yh", "z", "core")
ALL_AXES = DP + ("shard",)


def device_on(axis, index):
    return tuple(index if a == axis else lax.axis_index(a) for a in ALL_AXES)


def gather_kernel(axis, n, part, x_ref, out_ref, send_sem, recv_sem):
    me = lax.axis_index(axis)

    barrier = pltpu.get_barrier_semaphore()
    for off in range(1, n):
        peer = lax.rem(me + off, n)
        pl.semaphore_signal(barrier, inc=1, device_id=device_on(axis, peer), device_id_type=MESH)
    pl.semaphore_wait(barrier, n - 1)

    copies = []
    for off in range(1, n):
        peer = lax.rem(me + off, n)
        copy = pltpu.make_async_remote_copy(
            src_ref=x_ref.at[part],
            dst_ref=out_ref.at[me],
            send_sem=send_sem.at[off - 1],
            recv_sem=recv_sem.at[me],
            device_id=device_on(axis, peer),
            device_id_type=MESH,
        )
        copy.start()
        copies.append(copy)
    for copy in copies:
        copy.wait_send()
    for off in range(1, n):
        src = lax.rem(me + n - off, n)
        arrival = pltpu.make_async_remote_copy(
            src_ref=x_ref.at[part],
            dst_ref=out_ref.at[src],
            send_sem=send_sem.at[off - 1],
            recv_sem=recv_sem.at[src],
            device_id=device_on(axis, src),
            device_id_type=MESH,
        )
        arrival.wait_recv()


def gather_along(x, axis, collective_id):
    n = lax.axis_size(axis)
    received = pl.pallas_call(
        functools.partial(gather_kernel, axis, n, 0),
        out_shape=jax.ShapeDtypeStruct((n,) + x.shape, x.dtype),
        in_specs=[pl.BlockSpec(memory_space=pl.ANY)],
        out_specs=pl.BlockSpec(memory_space=pl.ANY),
        scratch_shapes=[pltpu.SemaphoreType.DMA((n - 1,)), pltpu.SemaphoreType.DMA((n,))],
        compiler_params=pltpu.CompilerParams(collective_id=collective_id, has_side_effects=True),
    )(x[None])
    whole = lax.dynamic_update_index_in_dim(received, x, lax.axis_index(axis), 0)
    return whole.reshape((n * x.shape[0],) + x.shape[1:])


def placed_gather_kernel(n, n_zhi, part, x_ref, out_ref, send_sem, recv_sem):
    me = lax.axis_index("shard")

    def where(j):
        return out_ref.at[:, pl.ds(2 * lax.rem(j, n_zhi), 2), pl.ds(j // n_zhi, 1)]

    barrier = pltpu.get_barrier_semaphore()
    for off in range(1, n):
        peer = lax.rem(me + off, n)
        pl.semaphore_signal(barrier, inc=1, device_id=device_on("shard", peer), device_id_type=MESH)
    pl.semaphore_wait(barrier, n - 1)

    copies = []
    for off in range(1, n):
        peer = lax.rem(me + off, n)
        copy = pltpu.make_async_remote_copy(
            src_ref=x_ref.at[part],
            dst_ref=where(me),
            send_sem=send_sem.at[off - 1],
            recv_sem=recv_sem.at[me],
            device_id=device_on("shard", peer),
            device_id_type=MESH,
        )
        copy.start()
        copies.append(copy)
    for copy in copies:
        copy.wait_send()
    for off in range(1, n):
        src = lax.rem(me + n - off, n)
        arrival = pltpu.make_async_remote_copy(
            src_ref=x_ref.at[part],
            dst_ref=where(src),
            send_sem=send_sem.at[off - 1],
            recv_sem=recv_sem.at[src],
            device_id=device_on("shard", src),
            device_id_type=MESH,
        )
        arrival.wait_recv()


def gather_part(xt, part, collective_id, out_dims):
    n = lax.axis_size("shard")
    n_zhi = out_dims[1] // 2
    received = pl.pallas_call(
        functools.partial(placed_gather_kernel, n, n_zhi, part),
        out_shape=jax.ShapeDtypeStruct(out_dims, xt.dtype),
        in_specs=[pl.BlockSpec(memory_space=pl.ANY)],
        out_specs=pl.BlockSpec(memory_space=pl.ANY),
        scratch_shapes=[pltpu.SemaphoreType.DMA((n - 1,)), pltpu.SemaphoreType.DMA((n,))],
        compiler_params=pltpu.CompilerParams(collective_id=collective_id, has_side_effects=True),
        cost_estimate=pl.CostEstimate(
            flops=0, bytes_accessed=2 * n * xt[part].nbytes, transcendentals=0
        ),
    )(xt)
    me = lax.axis_index("shard")
    at = (0, 2 * lax.rem(me, n_zhi), me // n_zhi, 0, 0)
    return lax.dynamic_update_slice(received, xt[part], at)


def swap_kernel(axis, halves, x_ref, out_ref, send_sem, recv_sem):
    me = lax.axis_index(axis)
    partner = device_on(axis, 1 - me)

    barrier = pltpu.get_barrier_semaphore()
    pl.semaphore_signal(barrier, inc=1, device_id=partner, device_id_type=MESH)
    pl.semaphore_wait(barrier, 1)

    copy = pltpu.make_async_remote_copy(
        src_ref=x_ref.at[1 - me] if halves else x_ref,
        dst_ref=out_ref,
        send_sem=send_sem,
        recv_sem=recv_sem,
        device_id=partner,
        device_id_type=MESH,
    )
    copy.start()
    copy.wait()


def swap_with_partner(x, collective_id, halves, axis="core"):
    return pl.pallas_call(
        functools.partial(swap_kernel, axis, halves),
        out_shape=jax.ShapeDtypeStruct(x.shape[1:] if halves else x.shape, x.dtype),
        in_specs=[pl.BlockSpec(memory_space=pl.ANY)],
        out_specs=pl.BlockSpec(memory_space=pl.ANY),
        scratch_shapes=[pltpu.SemaphoreType.DMA(()), pltpu.SemaphoreType.DMA(())],
        compiler_params=pltpu.CompilerParams(collective_id=collective_id, has_side_effects=True),
    )(x)


def ring_gather_kernel(axis, n, x_ref, both_ref, send_sem, recv_sem, pair_send, pair_recv):
    me = lax.axis_index(axis)
    out_ref = both_ref.at[lax.axis_index("core")]
    right, left = lax.rem(me + 1, n), lax.rem(me + n - 1, n)
    partner = device_on("core", 1 - lax.axis_index("core"))

    barrier = pltpu.get_barrier_semaphore()
    for neighbour in (left, right):
        pl.semaphore_signal(barrier, inc=1, device_id=device_on(axis, neighbour), device_id_type=MESH)
    pl.semaphore_signal(barrier, inc=1, device_id=partner, device_id_type=MESH)
    pl.semaphore_wait(barrier, 3)

    def arrival(slot):
        return pltpu.make_async_remote_copy(
            src_ref=x_ref,
            dst_ref=out_ref.at[slot],
            send_sem=send_sem.at[0, 0],
            recv_sem=recv_sem.at[slot],
            device_id=device_on(axis, left),
            device_id_type=MESH,
        )

    def to_partner(src, slot):
        return pltpu.make_async_remote_copy(
            src_ref=src,
            dst_ref=out_ref.at[slot],
            send_sem=pair_send.at[slot],
            recv_sem=pair_recv.at[slot],
            device_id=partner,
            device_id_type=MESH,
        )

    copies = []
    own = to_partner(x_ref, me)
    own.start()
    copies.append(own)
    steps = (n // 2, (n - 1) // 2)
    for k in range(max(steps)):
        for ring, (sign, target) in enumerate(((-1, right), (1, left))):
            if k >= steps[ring]:
                continue
            slot = lax.rem(me + sign * k + n, n)
            if k > 0:
                arrival(slot).wait_recv()
                forward = to_partner(out_ref.at[slot], slot)
                forward.start()
                copies.append(forward)
            copy = pltpu.make_async_remote_copy(
                src_ref=x_ref if k == 0 else out_ref.at[slot],
                dst_ref=out_ref.at[slot],
                send_sem=send_sem.at[ring, k],
                recv_sem=recv_sem.at[slot],
                device_id=device_on(axis, target),
                device_id_type=MESH,
            )
            copy.start()
            copies.append(copy)
    for slot in (lax.rem(me - steps[0] + n, n), lax.rem(me + steps[1], n)):
        arrival(slot).wait_recv()
        forward = to_partner(out_ref.at[slot], slot)
        forward.start()
        copies.append(forward)
    for copy in copies:
        copy.wait_send()
    theirs = both_ref.at[1 - lax.axis_index("core")]
    for slot in range(n):
        pltpu.make_async_remote_copy(
            src_ref=x_ref,
            dst_ref=theirs.at[slot],
            send_sem=pair_send.at[slot],
            recv_sem=pair_recv.at[slot],
            device_id=partner,
            device_id_type=MESH,
        ).wait_recv()


def ring_gather(x, axis, collective_id):
    n = lax.axis_size(axis)
    received = pl.pallas_call(
        functools.partial(ring_gather_kernel, axis, n),
        out_shape=jax.ShapeDtypeStruct((2, n) + x.shape, x.dtype),
        in_specs=[pl.BlockSpec(memory_space=pl.ANY)],
        out_specs=pl.BlockSpec(memory_space=pl.ANY),
        scratch_shapes=[
            pltpu.SemaphoreType.DMA((2, n // 2)),
            pltpu.SemaphoreType.DMA((n,)),
            pltpu.SemaphoreType.DMA((n,)),
            pltpu.SemaphoreType.DMA((n,)),
        ],
        compiler_params=pltpu.CompilerParams(collective_id=collective_id, has_side_effects=True),
    )(x)
    at = (lax.axis_index("core"), lax.axis_index(axis), 0, 0)
    whole = lax.dynamic_update_slice(received, x[None, None], at)
    return whole.reshape((2, n * x.shape[0]) + x.shape[1:])


def per_device(resid_in, hidden, w_down, frozen, steer, forget_flags):
    n_yh, n_z, n_c = (lax.axis_size(a) for a in DP)
    tok_rows, d_cols = resid_in.shape
    own_tokens, ff_rows = hidden.shape
    n_parts = 2
    sub = tok_rows // n_parts
    blocks = own_tokens // tok_rows
    total_tokens = own_tokens * lax.axis_size("shard")
    me_c = lax.axis_index("core")
    me_yh = lax.axis_index("yh")
    xt = hidden.reshape(blocks // n_c, n_c, n_parts, 1, sub, ff_rows).transpose(2, 1, 0, 3, 4, 5)
    hp_parts, mlp_parts = [], []
    pair_w = jnp.concatenate([w_down, swap_with_partner(w_down, 9, False)], axis=0)
    for part in range(n_parts):
        if part > 0:
            xt, _ = lax.optimization_barrier((xt, reduced))
        got = gather_part(xt, part, 2 * part, (n_c, n_z, n_yh, sub, ff_rows))
        hp = got.reshape(n_c, n_z * n_yh * sub, ff_rows)
        hp_parts.append(hp)
        from_partner = swap_with_partner(hp, 2 * part + 1, True)
        pair_rows = jnp.concatenate([hp[me_c], from_partner], axis=1)
        reduced = jnp.dot(pair_rows, pair_w, preferred_element_type=jnp.float32)
        reduced_z = lax.psum_scatter(reduced, "z", scatter_dimension=0, tiled=True)
        by_yh = reduced_z.reshape((n_yh, -1, d_cols))
        mlp_parts.append(by_yh[me_yh] + swap_with_partner(by_yh, 6 + part, True, "yh"))
    mlp_out = jnp.concatenate(mlp_parts, axis=0)
    residual = resid_in.astype(jnp.float32) + mlp_out
    updated = residual.astype(jnp.bfloat16)
    target_rows = lax.all_to_all(frozen, "shard", split_axis=1, concat_axis=0, tiled=True)
    row_block = (lax.axis_index("yh") * n_z + lax.axis_index("z")) * n_c + me_c
    start_row = row_block * tok_rows
    seq_ids = (start_row + jnp.arange(tok_rows, dtype=jnp.int32)) // SEQ_LEN
    seq_match = seq_ids[:, None] == jnp.arange(forget_flags.shape[0], dtype=jnp.int32)[None, :]
    is_forget = jnp.sum(jnp.where(seq_match, forget_flags[None, :], 0), axis=1) > 0
    target = jnp.where(
        is_forget[:, None], steer.astype(jnp.float32)[None, :], target_rows.astype(jnp.float32)
    )
    loss_weight = jnp.where(is_forget, 1.0, retain_weight).astype(jnp.float32)
    slopes = (loss_weight[:, None] * (residual - target) * (1.0 / math.sqrt(total_tokens))).astype(
        jnp.bfloat16
    )
    gathered = gather_along(slopes, "yh", 6 + n_parts)
    both = ring_gather(gathered, "z", 10).reshape(n_c, n_z * n_yh, n_parts, sub, d_cols)
    contract = (((0, 1), (0, 1)), ((), ()))
    grad_down = None
    for part in range(n_parts):
        term = lax.dot_general(
            hp_parts[part],
            both[:, :, part].reshape(n_c, -1, d_cols),
            contract,
            preferred_element_type=jnp.float32,
        )
        grad_down = term if grad_down is None else grad_down + term
    return (updated, grad_down)


def solution(mesh):
    n_dp, n_shard = mesh.devices.shape
    n_z = 8
    parts = mesh.devices.reshape(n_dp // (2 * n_z), n_z, 2, n_shard)
    split_mesh = Mesh(parts, DP + ("shard",))
    in_specs = (
        P(DP, "shard"),
        P("shard", DP),
        P(DP, "shard"),
        P(DP + ("shard",), None),
        P("shard"),
        P(),
    )
    out_specs = (P(DP, "shard"), P(DP, "shard"))
    return jax.shard_map(
        per_device, mesh=split_mesh, in_specs=in_specs, out_specs=out_specs, check_vma=False
    )
```

```python
import functools
import math

import jax
import jax.numpy as jnp
from jax import lax
from jax.experimental import pallas as pl
from jax.experimental.pallas import tpu as pltpu
from jax.sharding import Mesh, PartitionSpec as P

SEQ_LEN = 256
MESH = pl.DeviceIdType.MESH


retain_weight = 2.0


DP = ("yh", "z", "core")
ALL_AXES = DP + ("shard",)


def device_on(axis, index):
    return tuple(index if a == axis else lax.axis_index(a) for a in ALL_AXES)


def gather_kernel(axis, n, part, x_ref, out_ref, send_sem, recv_sem):
    me = lax.axis_index(axis)

    barrier = pltpu.get_barrier_semaphore()
    for off in range(1, n):
        peer = lax.rem(me + off, n)
        pl.semaphore_signal(barrier, inc=1, device_id=device_on(axis, peer), device_id_type=MESH)
    pl.semaphore_wait(barrier, n - 1)

    copies = []
    for off in range(1, n):
        peer = lax.rem(me + off, n)
        copy = pltpu.make_async_remote_copy(
            src_ref=x_ref.at[part],
            dst_ref=out_ref.at[me],
            send_sem=send_sem.at[off - 1],
            recv_sem=recv_sem.at[me],
            device_id=device_on(axis, peer),
            device_id_type=MESH,
        )
        copy.start()
        copies.append(copy)
    for copy in copies:
        copy.wait_send()
    for off in range(1, n):
        src = lax.rem(me + n - off, n)
        arrival = pltpu.make_async_remote_copy(
            src_ref=x_ref.at[part],
            dst_ref=out_ref.at[src],
            send_sem=send_sem.at[off - 1],
            recv_sem=recv_sem.at[src],
            device_id=device_on(axis, src),
            device_id_type=MESH,
        )
        arrival.wait_recv()


def gather_along(x, axis, collective_id):
    n = lax.axis_size(axis)
    received = pl.pallas_call(
        functools.partial(gather_kernel, axis, n, 0),
        out_shape=jax.ShapeDtypeStruct((n,) + x.shape, x.dtype),
        in_specs=[pl.BlockSpec(memory_space=pl.ANY)],
        out_specs=pl.BlockSpec(memory_space=pl.ANY),
        scratch_shapes=[pltpu.SemaphoreType.DMA((n - 1,)), pltpu.SemaphoreType.DMA((n,))],
        compiler_params=pltpu.CompilerParams(collective_id=collective_id, has_side_effects=True),
    )(x[None])
    whole = lax.dynamic_update_index_in_dim(received, x, lax.axis_index(axis), 0)
    return whole.reshape((n * x.shape[0],) + x.shape[1:])


def placed_gather_kernel(n, n_zhi, part, x_ref, out_ref, send_sem, recv_sem):
    me = lax.axis_index("shard")
    n_c = out_ref.shape[0]

    def where(j, c):
        return out_ref.at[c, pl.ds(2 * lax.rem(j, n_zhi), 2), pl.ds(j // n_zhi, 1)]

    barrier = pltpu.get_barrier_semaphore()
    for off in range(1, n):
        peer = lax.rem(me + off, n)
        pl.semaphore_signal(barrier, inc=1, device_id=device_on("shard", peer), device_id_type=MESH)
    pl.semaphore_wait(barrier, n - 1)

    def transfer(off, c, dest, slot):
        return pltpu.make_async_remote_copy(
            src_ref=x_ref.at[:, c, part],
            dst_ref=where(slot, c),
            send_sem=send_sem.at[off - 1, c],
            recv_sem=recv_sem.at[slot, c],
            device_id=device_on("shard", dest),
            device_id_type=MESH,
        )

    copies = []
    for off in range(1, n):
        for c in range(n_c):
            copy = transfer(off, c, lax.rem(me + off, n), me)
            copy.start()
            copies.append(copy)
    for copy in copies:
        copy.wait_send()
    for off in range(1, n):
        src = lax.rem(me + n - off, n)
        for c in range(n_c):
            transfer(off, c, src, src).wait_recv()


def gather_part(x6, part, collective_id, out_dims):
    n = lax.axis_size("shard")
    n_c, n_zhi = out_dims[0], out_dims[1] // 2
    received = pl.pallas_call(
        functools.partial(placed_gather_kernel, n, n_zhi, part),
        out_shape=jax.ShapeDtypeStruct(out_dims, x6.dtype),
        in_specs=[pl.BlockSpec(memory_space=pl.ANY)],
        out_specs=pl.BlockSpec(memory_space=pl.ANY),
        scratch_shapes=[pltpu.SemaphoreType.DMA((n - 1, n_c)), pltpu.SemaphoreType.DMA((n, n_c))],
        compiler_params=pltpu.CompilerParams(collective_id=collective_id, has_side_effects=True),
        cost_estimate=pl.CostEstimate(
            flops=0, bytes_accessed=2 * n * x6[:, :, part].nbytes, transcendentals=0
        ),
    )(x6)
    me = lax.axis_index("shard")
    at = (0, 2 * lax.rem(me, n_zhi), me // n_zhi, 0, 0)
    return lax.dynamic_update_slice(received, x6[:, :, part].swapaxes(0, 1), at)


def swap_kernel(axis, halves, x_ref, out_ref, send_sem, recv_sem):
    me = lax.axis_index(axis)
    partner = device_on(axis, 1 - me)

    barrier = pltpu.get_barrier_semaphore()
    pl.semaphore_signal(barrier, inc=1, device_id=partner, device_id_type=MESH)
    pl.semaphore_wait(barrier, 1)

    copy = pltpu.make_async_remote_copy(
        src_ref=x_ref.at[1 - me] if halves else x_ref,
        dst_ref=out_ref,
        send_sem=send_sem,
        recv_sem=recv_sem,
        device_id=partner,
        device_id_type=MESH,
    )
    copy.start()
    copy.wait()


def swap_with_partner(x, collective_id, halves, axis="core"):
    return pl.pallas_call(
        functools.partial(swap_kernel, axis, halves),
        out_shape=jax.ShapeDtypeStruct(x.shape[1:] if halves else x.shape, x.dtype),
        in_specs=[pl.BlockSpec(memory_space=pl.ANY)],
        out_specs=pl.BlockSpec(memory_space=pl.ANY),
        scratch_shapes=[pltpu.SemaphoreType.DMA(()), pltpu.SemaphoreType.DMA(())],
        compiler_params=pltpu.CompilerParams(collective_id=collective_id, has_side_effects=True),
    )(x)


def ring_gather_kernel(axis, n, x_ref, both_ref, send_sem, recv_sem, pair_send, pair_recv):
    me = lax.axis_index(axis)
    out_ref = both_ref.at[lax.axis_index("core")]
    right, left = lax.rem(me + 1, n), lax.rem(me + n - 1, n)
    partner = device_on("core", 1 - lax.axis_index("core"))

    barrier = pltpu.get_barrier_semaphore()
    for neighbour in (left, right):
        pl.semaphore_signal(barrier, inc=1, device_id=device_on(axis, neighbour), device_id_type=MESH)
    pl.semaphore_signal(barrier, inc=1, device_id=partner, device_id_type=MESH)
    pl.semaphore_wait(barrier, 3)

    def arrival(slot):
        return pltpu.make_async_remote_copy(
            src_ref=x_ref,
            dst_ref=out_ref.at[slot],
            send_sem=send_sem.at[0, 0],
            recv_sem=recv_sem.at[slot],
            device_id=device_on(axis, left),
            device_id_type=MESH,
        )

    def to_partner(src, slot):
        return pltpu.make_async_remote_copy(
            src_ref=src,
            dst_ref=out_ref.at[slot],
            send_sem=pair_send.at[slot],
            recv_sem=pair_recv.at[slot],
            device_id=partner,
            device_id_type=MESH,
        )

    copies = []
    own = to_partner(x_ref, me)
    own.start()
    copies.append(own)
    steps = (n // 2, (n - 1) // 2)
    for k in range(max(steps)):
        for ring, (sign, target) in enumerate(((-1, right), (1, left))):
            if k >= steps[ring]:
                continue
            slot = lax.rem(me + sign * k + n, n)
            if k > 0:
                arrival(slot).wait_recv()
                forward = to_partner(out_ref.at[slot], slot)
                forward.start()
                copies.append(forward)
            copy = pltpu.make_async_remote_copy(
                src_ref=x_ref if k == 0 else out_ref.at[slot],
                dst_ref=out_ref.at[slot],
                send_sem=send_sem.at[ring, k],
                recv_sem=recv_sem.at[slot],
                device_id=device_on(axis, target),
                device_id_type=MESH,
            )
            copy.start()
            copies.append(copy)
    for slot in (lax.rem(me - steps[0] + n, n), lax.rem(me + steps[1], n)):
        arrival(slot).wait_recv()
        forward = to_partner(out_ref.at[slot], slot)
        forward.start()
        copies.append(forward)
    for copy in copies:
        copy.wait_send()
    theirs = both_ref.at[1 - lax.axis_index("core")]
    for slot in range(n):
        pltpu.make_async_remote_copy(
            src_ref=x_ref,
            dst_ref=theirs.at[slot],
            send_sem=pair_send.at[slot],
            recv_sem=pair_recv.at[slot],
            device_id=partner,
            device_id_type=MESH,
        ).wait_recv()


def ring_gather(x, axis, collective_id):
    n = lax.axis_size(axis)
    received = pl.pallas_call(
        functools.partial(ring_gather_kernel, axis, n),
        out_shape=jax.ShapeDtypeStruct((2, n) + x.shape, x.dtype),
        in_specs=[pl.BlockSpec(memory_space=pl.ANY)],
        out_specs=pl.BlockSpec(memory_space=pl.ANY),
        scratch_shapes=[
            pltpu.SemaphoreType.DMA((2, n // 2)),
            pltpu.SemaphoreType.DMA((n,)),
            pltpu.SemaphoreType.DMA((n,)),
            pltpu.SemaphoreType.DMA((n,)),
        ],
        compiler_params=pltpu.CompilerParams(collective_id=collective_id, has_side_effects=True),
    )(x)
    at = (lax.axis_index("core"), lax.axis_index(axis), 0, 0)
    whole = lax.dynamic_update_slice(received, x[None, None], at)
    return whole.reshape((2, n * x.shape[0]) + x.shape[1:])


def per_device(resid_in, hidden, w_down, frozen, steer, forget_flags):
    n_yh, n_z, n_c = (lax.axis_size(a) for a in DP)
    tok_rows, d_cols = resid_in.shape
    own_tokens, ff_rows = hidden.shape
    n_parts = 2
    sub = tok_rows // n_parts
    blocks = own_tokens // tok_rows
    total_tokens = own_tokens * lax.axis_size("shard")
    me_c = lax.axis_index("core")
    me_yh = lax.axis_index("yh")
    xt = hidden.reshape(blocks // n_c, n_c, n_parts, 1, sub, ff_rows)
    hp_parts, mlp_parts = [], []
    pair_w = jnp.concatenate([w_down, swap_with_partner(w_down, 9, False)], axis=0)
    for part in range(n_parts):
        if part > 0:
            xt, _ = lax.optimization_barrier((xt, reduced))
        got = gather_part(xt, part, 2 * part, (n_c, n_z, n_yh, sub, ff_rows))
        hp = got.reshape(n_c, n_z * n_yh * sub, ff_rows)
        hp_parts.append(hp)
        from_partner = swap_with_partner(hp, 2 * part + 1, True)
        pair_rows = jnp.concatenate([hp[me_c], from_partner], axis=1)
        reduced = jnp.dot(pair_rows, pair_w, preferred_element_type=jnp.float32)
        reduced_z = lax.psum_scatter(reduced, "z", scatter_dimension=0, tiled=True)
        by_yh = reduced_z.reshape((n_yh, -1, d_cols))
        mlp_parts.append(by_yh[me_yh] + swap_with_partner(by_yh, 6 + part, True, "yh"))
    mlp_out = jnp.concatenate(mlp_parts, axis=0)
    residual = resid_in.astype(jnp.float32) + mlp_out
    updated = residual.astype(jnp.bfloat16)
    target_rows = lax.all_to_all(frozen, "shard", split_axis=1, concat_axis=0, tiled=True)
    row_block = (lax.axis_index("yh") * n_z + lax.axis_index("z")) * n_c + me_c
    start_row = row_block * tok_rows
    seq_ids = (start_row + jnp.arange(tok_rows, dtype=jnp.int32)) // SEQ_LEN
    seq_match = seq_ids[:, None] == jnp.arange(forget_flags.shape[0], dtype=jnp.int32)[None, :]
    is_forget = jnp.sum(jnp.where(seq_match, forget_flags[None, :], 0), axis=1) > 0
    target = jnp.where(
        is_forget[:, None], steer.astype(jnp.float32)[None, :], target_rows.astype(jnp.float32)
    )
    loss_weight = jnp.where(is_forget, 1.0, retain_weight).astype(jnp.float32)
    slopes = (loss_weight[:, None] * (residual - target) * (1.0 / math.sqrt(total_tokens))).astype(
        jnp.bfloat16
    )
    gathered = gather_along(slopes, "yh", 6 + n_parts)
    both = ring_gather(gathered, "z", 10).reshape(n_c, n_z * n_yh, n_parts, sub, d_cols)
    contract = (((0, 1), (0, 1)), ((), ()))
    grad_down = None
    for part in range(n_parts):
        term = lax.dot_general(
            hp_parts[part],
            both[:, :, part].reshape(n_c, -1, d_cols),
            contract,
            preferred_element_type=jnp.float32,
        )
        grad_down = term if grad_down is None else grad_down + term
    return (updated, grad_down)


def solution(mesh):
    n_dp, n_shard = mesh.devices.shape
    n_z = 8
    parts = mesh.devices.reshape(n_dp // (2 * n_z), n_z, 2, n_shard)
    split_mesh = Mesh(parts, DP + ("shard",))
    in_specs = (
        P(DP, "shard"),
        P("shard", DP),
        P(DP, "shard"),
        P(DP + ("shard",), None),
        P("shard"),
        P(),
    )
    out_specs = (P(DP, "shard"), P(DP, "shard"))
    return jax.shard_map(
        per_device, mesh=split_mesh, in_specs=in_specs, out_specs=out_specs, check_vma=False
    )
```
